32 devices in a mesh: gx: 4 (over y, x), gy: 8 (over z, core).
Axes of the slice: x: 2, y: 2, z: 4, core: 2. Of those that a mesh axis runs over, the one named last changes fastest.
Arguments:
- selectors: float32 [3, 8, 4, 8, 65536], P(None, None, 'gx', 'gy'), may hold values from 0 to 2047, as said below
- proofs: float32 [3, 8, 4, 8, 65536], P(None, None, 'gx', 'gy'), may hold values from 0 to 2047, as said below
- challenges: int32 [4], replicated, may hold values from 0 to 2147483646
Outputs:
- round_values: float32 [3, 4, 3], replicated
- folded_selectors: float32 [3, 8, 4, 8, 4096], P(None, None, 'gx', 'gy')
- folded_proofs: float32 [3, 8, 4, 8, 4096], P(None, None, 'gx', 'gy')
The draws below stay inside these ranges and needn't reach their ends.
Inputs may be any that keep to these rules, and one draw needn't show every extreme that they name: `selectors`: limbs of field elements, as in the first step. `proofs`: limbs of field elements, as in the first step. `challenges`: field elements.
All inputs are finite; a program needn't handle non-finite values.
Results may differ from the reference program's by a relative error of at most 0.0003.
Values sent between devices are 32-bit elements; how exact they have to be, the bound alone decides.
No kernel may reach another device: no remote copies, remote signals or barrier semaphores. Data moves between devices by JAX's collectives and lax.ppermute only.
A program may use at most 128 MiB of HBM per device.

```python
import jax
import jax.numpy as jnp
from jax import lax

PAIRS = 8
ROUNDS = 4
ROWS = 65536
XSPLIT = 4
YSPLIT = 8


def table_limbs(key):
    values = jax.random.randint(key, (PAIRS, XSPLIT, YSPLIT, ROWS), 0, 2147483647, dtype=jnp.int32)
    return jnp.stack([values & 2047, values >> 11 & 2047, values >> 22]).astype(jnp.float32)


def draw_selectors(key, part):
    return table_limbs(jax.random.fold_in(key, 11))


def draw_proofs(key, part):
    return table_limbs(jax.random.fold_in(key, 23))


def set_ends(values, key, low, top_value):
    longest = values.shape.index(max(values.shape))
    spots = []
    for shift in (0, 1):
        where = [jax.random.randint(jax.random.fold_in(key, axis), (), 0, length) for axis, length in enumerate(values.shape)]
        where[longest] = (where[longest] + shift) % values.shape[longest]
        spots.append(tuple(where))
    return values.at[spots[0]].set(low).at[spots[1]].set(top_value)


def setup_inputs(seed: int = 0) -> dict:
    key_list = jax.random.split(jax.random.key(seed), 4)
    selectors = draw_selectors(jax.random.fold_in(key_list[3], 71), 0)
    proofs = draw_proofs(jax.random.fold_in(key_list[3], 71), 0)
    challenges = set_ends(jax.random.randint(key_list[2], (ROUNDS,), 0, 2147483647), jax.random.fold_in(key_list[2], 1), 0, 2147483646).astype(jnp.int32)
    return {"selectors": selectors, "proofs": proofs, "challenges": challenges}


def settle(lowest, middle, highest):
    for repeat in range(3):
        carried = jnp.floor(lowest / 2048.0)
        lowest = lowest - carried * 2048.0
        middle = middle + carried
        carried = jnp.floor(middle / 2048.0)
        middle = middle - carried * 2048.0
        highest = highest + carried
        carried = jnp.floor(highest / 512.0)
        highest = highest - carried * 512.0
        lowest = lowest + carried
    at_modulus = (lowest == 2047.0) & (middle == 2047.0) & (highest == 511.0)
    nothing = jnp.zeros_like(lowest)
    return jnp.stack([jnp.where(at_modulus, nothing, lowest), jnp.where(at_modulus, nothing, middle), jnp.where(at_modulus, nothing, highest)])


def field_add(augend, addend):
    return settle(augend[0] + addend[0], augend[1] + addend[1], augend[2] + addend[2])


def field_sub(minuend, subtrahend):
    return settle(minuend[0] + 2047.0 - subtrahend[0], minuend[1] + 2047.0 - subtrahend[1], minuend[2] + 511.0 - subtrahend[2])


def field_mul(factor, multiplier):
    degree_zero = factor[0] * multiplier[0]
    degree_one = factor[0] * multiplier[1] + factor[1] * multiplier[0]
    degree_two = factor[0] * multiplier[2] + factor[1] * multiplier[1] + factor[2] * multiplier[0]
    degree_three = factor[1] * multiplier[2] + factor[2] * multiplier[1]
    degree_four = factor[2] * multiplier[2]
    carried = jnp.floor(degree_zero / 2048.0)
    degree_zero = degree_zero - carried * 2048.0
    degree_one = degree_one + carried
    carried = jnp.floor(degree_one / 2048.0)
    degree_one = degree_one - carried * 2048.0
    degree_two = degree_two + carried
    carried = jnp.floor(degree_two / 2048.0)
    degree_two = degree_two - carried * 2048.0
    degree_three = degree_three + carried
    carried = jnp.floor(degree_three / 2048.0)
    degree_three = degree_three - carried * 2048.0
    degree_four = degree_four + carried
    return settle(degree_zero + 4.0 * degree_three, degree_one + 4.0 * degree_four, degree_two)


def field_sum(values):
    values = values.reshape(3, -1)
    length = values.shape[1]
    while length > 1:
        stride = min(length, 2048)
        summed = values.reshape(3, length // stride, stride).sum(axis=2)
        values = settle(summed[0], summed[1], summed[2])
        length = length // stride
    return values.reshape(3)


def round_points(select_low, select_high, proof_low, proof_high):
    at_zero = field_sum(field_mul(select_low, proof_low))
    at_one = field_sum(field_mul(select_high, proof_high))
    select_two = field_sub(field_add(select_high, select_high), select_low)
    proof_two = field_sub(field_add(proof_high, proof_high), proof_low)
    at_two = field_sum(field_mul(select_two, proof_two))
    return jnp.stack([at_zero, at_one, at_two], axis=1)


def fold_tables(low_table, high_table, scalar):
    scalar = scalar.reshape((3,) + (1,) * (low_table.ndim - 1))
    return field_add(low_table, field_mul(field_sub(high_table, low_table), scalar))


def challenge_limbs(challenges, position):
    element = challenges[position]
    return jnp.stack([element & 2047, (element >> 11) & 2047, element >> 22]).astype(jnp.float32)


def split_top(values, position):
    shaped = values.shape
    reshaped = values.reshape(shaped[:position] + (2, shaped[position] // 2) + shaped[position + 1:])
    return lax.index_in_dim(reshaped, 0, position, keepdims=False), lax.index_in_dim(reshaped, 1, position, keepdims=False)


def reference(selectors, proofs, challenges):
    row_count = selectors.shape[-1]
    block_rows = min(row_count, 512)
    block_count = row_count // block_rows
    scalars = [challenge_limbs(challenges, position) for position in range(4)]
    shaped = (3, PAIRS, XSPLIT, YSPLIT, block_count, block_rows)
    select_blocks = jnp.transpose(selectors.reshape(shaped), (4, 0, 1, 2, 3, 5))
    proof_blocks = jnp.transpose(proofs.reshape(shaped), (4, 0, 1, 2, 3, 5))

    def one_block(tables):
        select_now, proof_now = tables
        points = []
        for round_index, position in enumerate([2, 2, 3, 3]):
            select_low, select_high = split_top(select_now, position)
            proof_low, proof_high = split_top(proof_now, position)
            points.append(round_points(select_low, select_high, proof_low, proof_high))
            select_now = fold_tables(select_low, select_high, scalars[round_index])
            proof_now = fold_tables(proof_low, proof_high, scalars[round_index])
        return jnp.stack(points, axis=1), select_now, proof_now

    points_all, select_done, proof_done = lax.map(one_block, (select_blocks, proof_blocks))
    summed = jnp.sum(points_all, axis=0)
    round_values = settle(summed[0], summed[1], summed[2])

    def arrange(done):
        rows_first = jnp.transpose(done, (1, 2, 3, 4, 0, 5)).reshape(3, PAIRS, XSPLIT // 4, YSPLIT // 4, row_count)
        blocks = rows_first.reshape(3, PAIRS, XSPLIT // 4, YSPLIT // 4, 4, 4, row_count // 16)
        return jnp.transpose(blocks, (0, 1, 4, 2, 5, 3, 6)).reshape(3, PAIRS, XSPLIT, YSPLIT, row_count // 16)

    return round_values, arrange(select_done), arrange(proof_done)
```

```python
import functools

import jax
import jax.numpy as jnp
from jax import lax
from jax.experimental import pallas as pl
from jax.experimental.pallas import tpu as pltpu
from jax.sharding import PartitionSpec as P


PRIME = 2147483647
LANES = 128


def shr(x, n):
    return lax.shift_right_logical(x, jnp.int32(n))


def reduce_once(x):
    return (x & PRIME) + shr(x, 31)


def add_mod(a, b):
    return reduce_once(a + b)


def sub_mod(a, b):
    return reduce_once(a + (PRIME - b))


def limbs_of(v):
    return v & 2047, shr(v, 11) & 2047, shr(v, 22)


def word_of_limbs(l0, l1, l2):
    half = jnp.floor(l2 * 0.5)
    base = (l0 + l1 * 2048.0) + ((l2 - half * 2.0) * 4194304.0 + 8388608.0)
    negative = half >= 128.0
    scale = jnp.exp2(half - jnp.where(negative, 192.0, 64.0))
    return base * jnp.where(negative, -scale, scale)


def word_of_int(v):
    base = ((v & 8388607) + 8388608).astype(jnp.float32)
    negative = v >= 1073741824
    scale = jnp.exp2(((shr(v, 23) & 127) - 64).astype(jnp.float32))
    return base * jnp.where(negative, -scale, scale)


def int_of_word(x):
    size = jnp.abs(x)
    level = jnp.floor(jnp.log2(size) + 0.0009765625)
    value = size * jnp.exp2(23.0 - level)
    over = value < 8388608.0
    value = jnp.where(over, value * 2.0, value)
    level = jnp.where(over, level - 1.0, level)
    offset = jnp.where(x < 0.0, jnp.int32((40 << 23) + (1 << 30)), jnp.int32(40 << 23))
    return value.astype(jnp.int32) + (level.astype(jnp.int32) << 23) + offset


def int_of_limbs(l0, l1, l2):
    return (l0 + l1 * 2048.0).astype(jnp.int32) + (l2.astype(jnp.int32) << 22)


def scale_mod(limbs, consts):
    a0, a1, a2 = limbs
    low = a0 * consts[0] + a1 * consts[1] + a2 * consts[2]
    high = a0 * consts[3] + a1 * consts[4] + a2 * consts[5]
    return reduce_once(low + ((high & 32767) << 16) + shr(high, 15))


def fold(own, other, consts):
    return add_mod(own, scale_mod(limbs_of(sub_mod(other, own)), consts))


def degrees(a, b):
    return [
        a[0] * b[0],
        a[0] * b[1] + a[1] * b[0],
        a[0] * b[2] + a[1] * b[1] + a[2] * b[0],
        a[1] * b[2] + a[2] * b[1],
        a[2] * b[2],
    ]


def round_degrees(s_own, s_other, w_own, w_other):
    so, st, wo, wt = limbs_of(s_own), limbs_of(s_other), limbs_of(w_own), limbs_of(w_other)
    sums = [x + y for x, y in zip(so, st)], [x + y for x, y in zip(wo, wt)]
    return degrees(so, wo) + degrees(st, wt) + degrees(*sums)


def rotate(x, n):
    return ((x << n) & PRIME) + shr(x, 31 - n)


def element_of_degrees(d):
    total = add_mod(d[0], rotate(d[1], 11))
    total = add_mod(total, rotate(d[2], 22))
    total = add_mod(total, rotate(d[3], 2))
    return add_mod(total, rotate(d[4], 13))


def put_points(points_ref, first, degree_sums):
    for kind in range(3):
        here = element_of_degrees(degree_sums[5 * kind : 5 * kind + 5])
        points_ref[first + kind] = add_mod(points_ref[first + kind], here)


def zeros15():
    return tuple(jnp.zeros((8, LANES), jnp.int32) for _ in range(15))


def consts_of(scalars_ref, which):
    return [scalars_ref[6 * which + i] for i in range(6)]


def encode_kernel(place_ref, *refs):
    ins, outs = refs[:6], refs[6:]
    for d in range(3):
        for t in range(2):
            src = ins[2 * d + t]
            outs[d][t, 0] = word_of_limbs(src[0, 0], src[1, 0], src[2, 0])


def first_kernel(place_ref, scalars_ref, s_ref, w_ref, g1, g2, g3, kept_ref, o1, o2, o3, points_ref, once):
    rows = s_ref.shape[2]
    sub = rows // 4
    given = (g1, g2, g3)
    outs = (kept_ref, o1, o2, o3)
    here = place_ref[1]

    @pl.when(pl.program_id(0) == 0)
    def _():
        points_ref[...] = jnp.zeros_like(points_ref)

    c_first, c_second = consts_of(scalars_ref, 0), consts_of(scalars_ref, 1)

    def round_one(i, acc):
        at = pl.ds(pl.multiple_of(i * 8, 8), 8)
        values = []
        for t, ref in ((0, s_ref), (1, w_ref)):
            own = int_of_limbs(ref[0, 0, at], ref[1, 0, at], ref[2, 0, at])
            values.append([own] + [int_of_word(g[t, 0, at]) for g in given])
        s, w = values
        d = [x + y for x, y in zip(round_degrees(s[0], s[2], w[0], w[2]), round_degrees(s[1], s[3], w[1], w[3]))]
        for t in range(2):
            v = values[t]
            once[t, 0, at] = fold(v[0], v[2], c_first)
            once[t, 1, at] = fold(v[1], v[3], c_first)
        return tuple(x + y for x, y in zip(acc, d))

    put_points(points_ref, 0, lax.fori_loop(0, rows // 8, round_one, zeros15()))

    acc = zeros15()
    for e in range(4):
        start = (here ^ e) * sub

        def round_two(i, acc):
            at = pl.ds(pl.multiple_of(start + i * 8, 8), 8)
            to = pl.ds(pl.multiple_of(i * 8, 8), 8)
            s, w = [[once[t, 0, at], once[t, 1, at]] for t in range(2)]
            d = round_degrees(s[0], s[1], w[0], w[1])
            for t, v in ((0, s), (1, w)):
                folded = fold(v[0], v[1], c_second)
                outs[e][t, 0, to] = folded if e == 0 else word_of_int(folded)
            return tuple(x + y for x, y in zip(acc, d))

        acc = lax.fori_loop(0, sub // 8, round_two, acc)
    put_points(points_ref, 3, acc)


def settle(lowest, middle, highest):
    for _ in range(3):
        carried = jnp.floor(lowest * (1.0 / 2048.0))
        lowest = lowest - carried * 2048.0
        middle = middle + carried
        carried = jnp.floor(middle * (1.0 / 2048.0))
        middle = middle - carried * 2048.0
        highest = highest + carried
        carried = jnp.floor(highest * (1.0 / 512.0))
        highest = highest - carried * 512.0
        lowest = lowest + carried
    at_modulus = (lowest == 2047.0) & (middle == 2047.0) & (highest == 511.0)
    return [jnp.where(at_modulus, 0.0, limb) for limb in (lowest, middle, highest)]


def publish_row(scalars_ref, points, sums_ref):
    lane = lax.broadcasted_iota(jnp.int32, (1, LANES), 1)
    rows = [jnp.zeros((1, LANES), jnp.float32) for _ in range(3)]
    for k in range(4):
        own, other, both = points[3 * k : 3 * k + 3]
        low_side = scalars_ref[24 + k] == 0
        at_zero = jnp.where(low_side, own, other)
        at_one = jnp.where(low_side, other, own)
        once = add_mod(at_zero, add_mod(at_one, at_one))
        at_two = sub_mod(add_mod(once, add_mod(once, once)), add_mod(both, both))
        for t, value in enumerate((at_zero, at_one, at_two)):
            for n, limb in enumerate(limbs_of(value)):
                total = jnp.sum(limb.astype(jnp.float32), axis=(0, 1), keepdims=True)
                rows[n] = jnp.where(lane == 3 * k + t, total, rows[n])
    low, mid, high = settle(*rows)
    packed = low + pltpu.roll(mid, 16, 1) + pltpu.roll(high, 32, 1)
    sums_ref[...] = jnp.broadcast_to(packed, sums_ref.shape)


def second_kernel(last, before, scalars_ref, kept_ref, g1, g2, g3, *refs):
    if last:
        earlier, refs = refs[: 2 * before + 1], refs[2 * before + 1 :]
        refs = refs[2:] if before else refs
        fs_ref, fw_ref, sums_ref, points_ref, once = refs
    else:
        refs = refs[2:] if before else refs
        fs_ref, fw_ref, points_ref, once = refs
    rows = kept_ref.shape[2]
    given = (g1, g2, g3)

    @pl.when(pl.program_id(0) == 0)
    def _():
        points_ref[...] = jnp.zeros_like(points_ref)

    c_first, c_second = consts_of(scalars_ref, 2), consts_of(scalars_ref, 3)

    def round_three(i, acc):
        at = pl.ds(pl.multiple_of(i * 8, 8), 8)
        values = [[kept_ref[t, 0, at]] + [int_of_word(g[t, 0, at]) for g in given] for t in range(2)]
        s, w = values
        d = [x + y for x, y in zip(round_degrees(s[0], s[2], w[0], w[2]), round_degrees(s[1], s[3], w[1], w[3]))]
        for t in range(2):
            v = values[t]
            once[t, 0, at] = fold(v[0], v[2], c_first)
            once[t, 1, at] = fold(v[1], v[3], c_first)
        return tuple(x + y for x, y in zip(acc, d))

    put_points(points_ref, 0, lax.fori_loop(0, rows // 8, round_three, zeros15()))

    def round_four(i, acc):
        at = pl.ds(pl.multiple_of(i * 8, 8), 8)
        s, w = [[once[t, 0, at], once[t, 1, at]] for t in range(2)]
        d = round_degrees(s[0], s[1], w[0], w[1])
        for out, v in ((fs_ref, s), (fw_ref, w)):
            folded = fold(v[0], v[1], c_second)
            folded = jnp.where(folded == PRIME, 0, folded)
            for n, limb in enumerate(limbs_of(folded)):
                out[n, 0, at] = limb.astype(jnp.float32)
        return tuple(x + y for x, y in zip(acc, d))

    put_points(points_ref, 3, lax.fori_loop(0, rows // 8, round_four, zeros15()))

    if last:

        @pl.when(pl.program_id(0) == pl.num_programs(0) - 1)
        def _():
            firsts, seconds = earlier[: before + 1], earlier[before + 1 :]
            points = []
            for k in range(6):
                total = firsts[0][k]
                for ref in firsts[1:]:
                    total = add_mod(total, ref[k])
                points.append(total)
            for k in range(6):
                total = points_ref[k]
                for ref in seconds:
                    total = add_mod(total, ref[k])
                points.append(total)
            publish_row(scalars_ref, points, sums_ref)


def swap_with(x, axis, mask):
    return lax.ppermute(x, axis, [(i, i ^ mask) for i in range(lax.axis_size(axis))])


def round_scalars(challenges, gx_place, gy_place):
    bits = jnp.stack([gx_place >> 1, gx_place & 1, gy_place >> 1, gy_place & 1])
    c = jnp.where(bits == 0, challenges, jnp.where(challenges == 0, 1, PRIME - challenges + 1))
    parts = [c, ((c << 11) & PRIME) | shr(c, 20), ((c << 22) & PRIME) | shr(c, 9)]
    table = jnp.stack([x & 65535 for x in parts] + [x >> 16 for x in parts], axis=1)
    return jnp.concatenate([table.reshape(24), bits]).astype(jnp.int32)


CHUNKS = (2, 2, 2, 2)


def shards(devices, selectors, proofs, challenges):
    polynomials, row_count = selectors.shape[1], selectors.shape[-1]
    lane_rows = row_count // LANES
    quarter, final = lane_rows // 4, lane_rows // 16
    tables = [x.reshape(3, polynomials, lane_rows, LANES) for x in (selectors, proofs)]
    gx_shift = lax.axis_size("gx").bit_length() - 3
    gy_shift = lax.axis_size("gy").bit_length() - 3
    gx_place = lax.axis_index("gx") >> gx_shift
    gy_place = lax.axis_index("gy") >> gy_shift
    place = jnp.stack([gx_place, gy_place]).astype(jnp.int32)
    scalars = round_scalars(challenges, gx_place, gy_place)

    sizes = CHUNKS if sum(CHUNKS) == polynomials else (1,) * polynomials
    starts = [sum(sizes[:c]) for c in range(len(sizes))]
    smem = pl.BlockSpec(memory_space=pltpu.SMEM)

    def words(count, rows, dtype=jnp.float32):
        return jax.ShapeDtypeStruct((2, count, rows, LANES), dtype)

    def word_spec(rows):
        return pl.BlockSpec((2, 1, rows, LANES), lambda j, *_: (0, j, 0, 0))

    points_shape = jax.ShapeDtypeStruct((6, 8, LANES), jnp.int32)
    points_spec = pl.BlockSpec((6, 8, LANES), lambda j, *_: (0, 0, 0))

    def encode(start, count):
        def spec(d):
            return pl.BlockSpec((3, 1, quarter, LANES), lambda j, place: (0, start + j, place[0] ^ d, 0))

        return pl.pallas_call(
            encode_kernel,
            grid_spec=pltpu.PrefetchScalarGridSpec(
                num_scalar_prefetch=1,
                grid=(count,),
                in_specs=[spec(d) for d in (1, 2, 3) for _ in range(2)],
                out_specs=[word_spec(quarter)] * 3,
            ),
            out_shape=[words(count, quarter)] * 3,
            name="encode",
        )(place, *(tables * 3))

    def first(start, count, given):
        table = pl.BlockSpec((3, 1, quarter, LANES), lambda j, place, scalars: (0, start + j, place[0], 0))
        return pl.pallas_call(
            first_kernel,
            grid_spec=pltpu.PrefetchScalarGridSpec(
                num_scalar_prefetch=2,
                grid=(count,),
                in_specs=[table] * 2 + [word_spec(quarter)] * 3,
                out_specs=[word_spec(final)] * 4 + [points_spec],
                scratch_shapes=[pltpu.VMEM((2, 2, quarter, LANES), jnp.int32)],
            ),
            out_shape=[words(count, final, jnp.int32)] + [words(count, final)] * 3 + [points_shape],
            name="first_rounds",
        )(place, scalars, *tables, *given)

    def second(start, count, kept, given, firsts, seconds, folded):
        last = start + count == polynomials
        before = len(seconds)
        extra, extra_specs = [], []
        if last:
            extra = list(firsts) + list(seconds)
            extra_specs = [points_spec] * len(extra)
        aliases = {}
        if before:
            base = 1 + 4 + len(extra)
            extra += list(folded)
            extra_specs += [pl.BlockSpec(memory_space=pl.ANY)] * 2
            aliases = {base: 0, base + 1: 1}
        out_spec = pl.BlockSpec((3, 1, final, LANES), lambda j, *_: (0, start + j, 0, 0))
        out_shape = [jax.ShapeDtypeStruct((3, polynomials, final, LANES), jnp.float32)] * 2
        out_specs = [out_spec] * 2
        scratch = [pltpu.VMEM((2, 2, final, LANES), jnp.int32)]
        if last:
            out_shape.append(jax.ShapeDtypeStruct((devices, 1, LANES), jnp.float32))
            out_specs.append(pl.BlockSpec((devices, 1, LANES), lambda j, *_: (0, 0, 0)))
            scratch = [pltpu.VMEM((6, 8, LANES), jnp.int32)] + scratch
        else:
            out_shape.append(points_shape)
            out_specs.append(points_spec)
        return pl.pallas_call(
            functools.partial(second_kernel, last, before),
            grid_spec=pltpu.PrefetchScalarGridSpec(
                num_scalar_prefetch=1,
                grid=(count,),
                in_specs=[word_spec(final)] * 4 + extra_specs,
                out_specs=out_specs,
                scratch_shapes=scratch,
            ),
            out_shape=out_shape,
            input_output_aliases=aliases,
            name="second_rounds",
        )(scalars, kept, *given, *extra)

    sent = []
    for start, count in zip(starts, sizes):
        given = encode(start, count)
        sent.append([swap_with(x, "gx", (d + 1) << gx_shift) for d, x in enumerate(given)])
    firsts, seconds, folded = [], [], None
    waiting = []
    for c, (start, count) in enumerate(zip(starts, sizes)):
        kept, *given, points = first(start, count, sent[c])
        firsts.append(points)
        waiting.append((kept, [swap_with(x, "gy", (e + 1) << gy_shift) for e, x in enumerate(given)]))
    for c, (start, count) in enumerate(zip(starts, sizes)):
        kept, given = waiting[c]
        *folded, out = second(start, count, kept, given, firsts, seconds, folded)
        seconds.append(out)
    gathered = lax.all_to_all(seconds[-1], ("gx", "gy"), 0, 0)
    total = gathered.sum(axis=0).reshape(LANES)
    points = jnp.stack(settle(total[0:12], total[16:28], total[32:44])).reshape(3, 4, 3)
    shape = (3, polynomials, 1, 1, row_count // 16)
    return points, folded[0].reshape(shape), folded[1].reshape(shape)


def solution(mesh):
    tables = P(None, None, "gx", "gy", None)
    devices = mesh.shape["gx"] * mesh.shape["gy"]
    return jax.shard_map(
        functools.partial(shards, devices),
        mesh=mesh,
        in_specs=(tables, tables, P()),
        out_specs=(P(), tables, tables),
        check_vma=False,
    )
```

```python
import functools

import jax
import jax.numpy as jnp
from jax import lax
from jax.experimental import pallas as pl
from jax.experimental.pallas import tpu as pltpu
from jax.sharding import PartitionSpec as P


PRIME = 2147483647
LANES = 128
VMEM_ENCODE, VMEM_KERNEL = 16 << 20, 8 << 20


def shr(x, n):
    return lax.shift_right_logical(x, jnp.int32(n))


def reduce_once(x):
    return (x & PRIME) + shr(x, 31)


def add_mod(a, b):
    return reduce_once(a + b)


def sub_mod(a, b):
    return reduce_once(a + (PRIME - b))


def limbs_of(v):
    return v & 2047, shr(v, 11) & 2047, shr(v, 22)


def word_of_limbs(l0, l1, l2):
    half = jnp.floor(l2 * 0.5)
    base = (l0 + l1 * 2048.0) + ((l2 - half * 2.0) * 4194304.0 + 8388608.0)
    negative = half >= 128.0
    scale = jnp.exp2(half - jnp.where(negative, 192.0, 64.0))
    return base * jnp.where(negative, -scale, scale)


def word_of_int(v):
    base = ((v & 8388607) + 8388608).astype(jnp.float32)
    negative = v >= 1073741824
    scale = jnp.exp2(((shr(v, 23) & 127) - 64).astype(jnp.float32))
    return base * jnp.where(negative, -scale, scale)


def int_of_word(x):
    size = jnp.abs(x)
    level = jnp.floor(jnp.log2(size) + 0.0009765625)
    value = size * jnp.exp2(23.0 - level)
    value = jnp.minimum(value, value + value - 8388608.0)
    offset = jnp.where(x < 0.0, jnp.int32((40 << 23) + (1 << 30)), jnp.int32(40 << 23))
    return value.astype(jnp.int32) + (level.astype(jnp.int32) << 23) + offset


def int_of_limbs(l0, l1, l2):
    return (l0 + l1 * 2048.0).astype(jnp.int32) + (l2.astype(jnp.int32) << 22)


def weighted_sum(limbs, weights):
    low = high = None
    for a, c in zip(limbs, weights):
        for n in range(3):
            low = a[n] * c[n] if low is None else low + a[n] * c[n]
            high = a[n] * c[3 + n] if high is None else high + a[n] * c[3 + n]
    return reduce_once(low + ((high & 32767) << 16) + shr(high, 15))


def degrees(a, b):
    return [
        a[0] * b[0],
        a[0] * b[1] + a[1] * b[0],
        a[0] * b[2] + a[1] * b[1] + a[2] * b[0],
        a[1] * b[2] + a[2] * b[1],
        a[2] * b[2],
    ]


def rotate(x, n):
    return ((x << n) & PRIME) + shr(x, 31 - n)


def element_of_degrees(d):
    total = add_mod(reduce_once(d[0]), rotate(d[1], 11))
    total = add_mod(total, rotate(d[2], 22))
    total = add_mod(total, rotate(d[3], 2))
    return add_mod(total, rotate(d[4], 13))


def mul_mod(a, b):
    return element_of_degrees(degrees(limbs_of(a), limbs_of(b)))


def add_limbs(a, b):
    return [x + y for x, y in zip(a, b)]


def nine_of(v):
    s02, s13 = add_limbs(v[0], v[2]), add_limbs(v[1], v[3])
    s01, s23 = add_limbs(v[0], v[1]), add_limbs(v[2], v[3])
    return [*v, s02, s13, s01, s23, add_limbs(s01, s23)]


def clear(acc_ref):
    for n in range(45):
        acc_ref[n] = jnp.zeros((8, LANES), jnp.int32)


def two_rounds(acc_ref, splat_ref, s, w):
    s, w = [[limbs_of(x) for x in v] for v in (s, w)]
    for kind, (a, b) in enumerate(zip(nine_of(s), nine_of(w))):
        for n, d in enumerate(degrees(a, b)):
            acc_ref[5 * kind + n] = acc_ref[5 * kind + n] + d
    weights = [[splat_ref[6 * x + n] for n in range(6)] for x in range(4)]
    return weighted_sum(s, weights), weighted_sum(w, weights)


def flush(acc_ref, points_ref, first):
    for kind in range(9):
        here = element_of_degrees([acc_ref[5 * kind + n] for n in range(5)])
        points_ref[first + kind] = add_mod(points_ref[first + kind], here)


def whole(scalar):
    return jnp.full((8, LANES), scalar, jnp.int32)


def sides(challenges_ref, place, phase):
    out = []
    for k in range(2):
        high = whole(challenges_ref[2 * phase + k])
        low = jnp.where(high == 0, 1, PRIME - high + 1)
        is_low = whole((place >> (1 - k)) & 1) == 0
        out.append((jnp.where(is_low, low, high), jnp.where(is_low, high, low)))
    return out


def constants_of(weight):
    parts = [weight, rotate(weight, 11), rotate(weight, 22)]
    return [x & 65535 for x in parts] + [shr(x, 16) for x in parts]


def splat_weights(challenges_ref, place, phase, splat_ref):
    first, second = sides(challenges_ref, place, phase)
    for x in range(4):
        for n, c in enumerate(constants_of(mul_mod(first[x >> 1], second[x & 1]))):
            splat_ref[6 * x + n] = c


def tile(start, i):
    return pl.ds(pl.multiple_of(start + i * 8, 8), 8)


def encode_kernel(start, place_ref, s_hbm, w_hbm, *refs):
    own_ref, o1, o2, o3, token_ref, buffer, sems = refs[-7:]
    count, rows = own_ref.shape[1], own_ref.shape[2]
    here = place_ref[0]
    order = [(j, d, t) for j in range(count) for d in (1, 2, 3, 0) for t in range(2)]

    def copy(j, d, t):
        src = (s_hbm, w_hbm)[t].at[:, start + j, pl.ds(pl.multiple_of((here ^ d) * rows, rows), rows), :]
        return pltpu.make_async_copy(src, buffer.at[j, d, t], sems.at[j, d, t])

    for where in order:
        copy(*where).start()
    token_ref[...] = jnp.zeros_like(token_ref)
    for where in order:
        j, d, t = where
        copy(*where).wait()

        def step(i, _):
            at = tile(0, i)
            limbs = [buffer[j, d, t, n, at] for n in range(3)]
            if d:
                (o1, o2, o3)[d - 1][t, j, at] = word_of_limbs(*limbs)
            else:
                own_ref[t, j, at] = int_of_limbs(*limbs)

        lax.fori_loop(0, rows // 8, step, None, unroll=4)


def first_kernel(fresh, challenges_ref, gx_ref, gy_ref, own_ref, g1, g2, g3, *refs):
    if not fresh:
        before_ref, *refs = refs
    points_ref, kept_ref, o1, o2, o3, acc_ref, splat_ref = refs
    count, rows = own_ref.shape[1], own_ref.shape[2]
    sub = rows // 4
    given, outs = (g1, g2, g3), (kept_ref, o1, o2, o3)
    splat_weights(challenges_ref, gx_ref[0], 0, splat_ref)
    points_ref[...] = jnp.zeros_like(points_ref) if fresh else before_ref[...]

    def pair(j, _):
        clear(acc_ref)
        for e in range(4):
            start = (gy_ref[0] ^ e) * sub

            def step(i, _):
                at = tile(start, i)
                s, w = [[own_ref[t, j, at]] + [int_of_word(g[t, j, at]) for g in given] for t in range(2)]
                for t, folded in enumerate(two_rounds(acc_ref, splat_ref, s, w)):
                    outs[e][t, j, tile(0, i)] = word_of_int(folded) if e else folded

            lax.fori_loop(0, sub // 8, step, None, unroll=2)
        flush(acc_ref, points_ref, 0)

    lax.fori_loop(0, count, pair, None)


def settle(lowest, middle, highest):
    for _ in range(3):
        carried = jnp.floor(lowest * (1.0 / 2048.0))
        lowest = lowest - carried * 2048.0
        middle = middle + carried
        carried = jnp.floor(middle * (1.0 / 2048.0))
        middle = middle - carried * 2048.0
        highest = highest + carried
        carried = jnp.floor(highest * (1.0 / 512.0))
        highest = highest - carried * 512.0
        lowest = lowest + carried
    at_modulus = (lowest == 2047.0) & (middle == 2047.0) & (highest == 511.0)
    return [jnp.where(at_modulus, 0.0, limb) for limb in (lowest, middle, highest)]


def round_sums(challenges_ref, place, phase, points):
    own, other = sides(challenges_ref, place, phase)[0]
    squares = [constants_of(mul_mod(*x)) for x in ((own, own), (own, other), (other, other))]
    i0, i1, i2, i3, i02, i13, i01, i23, i0123 = points
    first = [add_mod(i0, i1), add_mod(i2, i3), add_mod(i02, i13)]
    second = []
    for own, other, both in ((i0, i2, i02), (i1, i3, i13), (i01, i23, i0123)):
        cross = sub_mod(both, add_mod(own, other))
        second.append(weighted_sum([limbs_of(x) for x in (own, cross, other)], squares))
    return [first, second]


def publish_row(challenges_ref, places, points_ref, sums_ref):
    lane = lax.broadcasted_iota(jnp.int32, (1, LANES), 1)
    rows = [jnp.zeros((1, LANES), jnp.float32) for _ in range(3)]
    for phase in range(2):
        place = places[phase]
        points = [points_ref[9 * phase + n] for n in range(9)]
        for k, (own, other, both) in enumerate(round_sums(challenges_ref, place, phase, points)):
            is_low = whole((place >> (1 - k)) & 1) == 0
            at_zero = jnp.where(is_low, own, other)
            at_one = jnp.where(is_low, other, own)
            once = add_mod(at_zero, add_mod(at_one, at_one))
            at_two = sub_mod(add_mod(once, add_mod(once, once)), add_mod(both, both))
            for t, value in enumerate((at_zero, at_one, at_two)):
                for n, limb in enumerate(limbs_of(value)):
                    total = jnp.sum(limb.astype(jnp.float32), axis=(0, 1), keepdims=True)
                    rows[n] = jnp.where(lane == 6 * phase + 3 * k + t, total, rows[n])
    low, mid, high = settle(*rows)
    packed = low + pltpu.roll(mid, 16, 1) + pltpu.roll(high, 32, 1)
    sums_ref[...] = jnp.broadcast_to(packed, sums_ref.shape)


def second_kernel(start, fresh, last, challenges_ref, gx_ref, gy_ref, kept_ref, g1, g2, g3, before_ref, *refs):
    if not fresh:
        refs = refs[2:]
    points_ref, s_ref, w_ref, *refs = refs
    if last:
        sums_ref, s_hbm, w_hbm, *refs = refs
        sems = refs.pop()
    acc_ref, splat_ref = refs
    count, rows = kept_ref.shape[1], kept_ref.shape[2]
    given = (g1, g2, g3)

    def copies(which, part):
        return [
            pltpu.make_async_copy(src.at[:, part], dst.at[:, part], sems.at[which, t])
            for t, (src, dst) in enumerate(((s_ref, s_hbm), (w_ref, w_hbm)))
        ]

    if last and start:
        for copy in copies(0, pl.ds(0, start)):
            copy.start()
    splat_weights(challenges_ref, gy_ref[0], 1, splat_ref)
    points_ref[...] = before_ref[...]

    def pair(j, _):
        clear(acc_ref)

        def step(i, _):
            at = tile(0, i)
            s, w = [[kept_ref[t, j, at]] + [int_of_word(g[t, j, at]) for g in given] for t in range(2)]
            for out, folded in zip((s_ref, w_ref), two_rounds(acc_ref, splat_ref, s, w)):
                for n, limb in enumerate(limbs_of(jnp.where(folded == PRIME, 0, folded))):
                    out[n, start + j, at] = limb.astype(jnp.float32)

        lax.fori_loop(0, rows // 8, step, None, unroll=2)
        flush(acc_ref, points_ref, 9)

    lax.fori_loop(0, count, pair, None)
    if last:
        for copy in copies(1, pl.ds(start, count)):
            copy.start()
        publish_row(challenges_ref, (gx_ref[0], gy_ref[0]), points_ref, sums_ref)
        for copy in copies(1, pl.ds(start, count)) + (copies(0, pl.ds(0, start)) if start else []):
            copy.wait()


def swap_with(x, axis, mask):
    return lax.ppermute(x, axis, [(i, i ^ mask) for i in range(lax.axis_size(axis))])


CHUNKS = (3, 3, 2)
POINTS = pltpu.VMEM((18, 8, LANES), jnp.int32)


def shards(devices, selectors, proofs, challenges):
    polynomials, row_count = selectors.shape[1], selectors.shape[-1]
    lane_rows = row_count // LANES
    quarter, final = lane_rows // 4, lane_rows // 16
    tables = [
        pltpu.with_memory_space_constraint(x.reshape(3, polynomials, lane_rows, LANES), pltpu.HBM)
        for x in (selectors, proofs)
    ]
    gx_shift = lax.axis_size("gx").bit_length() - 3
    gy_shift = lax.axis_size("gy").bit_length() - 3
    gx_place = (lax.axis_index("gx") >> gx_shift).astype(jnp.int32).reshape(1)
    gy_place = (lax.axis_index("gy") >> gy_shift).astype(jnp.int32).reshape(1)

    sizes = CHUNKS if sum(CHUNKS) == polynomials else (1,) * polynomials
    starts = [sum(sizes[:c]) for c in range(len(sizes))]
    chunks = len(sizes)
    smem, vmem, hbm, anywhere = [pl.BlockSpec(memory_space=m) for m in (pltpu.SMEM, pltpu.VMEM, pltpu.HBM, pl.ANY)]

    def words(count, rows, dtype=jnp.float32):
        return pltpu.VMEM((2, count, rows, LANES), dtype)

    def near(arrays):
        return [pltpu.with_memory_space_constraint(x, pltpu.VMEM) for x in arrays]

    work = [pltpu.VMEM((45, 8, LANES), jnp.int32), pltpu.VMEM((24, 8, LANES), jnp.int32)]
    small = pltpu.CompilerParams(vmem_limit_bytes=VMEM_KERNEL)

    def encode(c, token):
        count = sizes[c]
        return pl.pallas_call(
            functools.partial(encode_kernel, starts[c]),
            in_specs=[smem, hbm, hbm] + [anywhere] * len(token),
            out_specs=[vmem] * 5,
            out_shape=[words(count, quarter, jnp.int32)] + [words(count, quarter)] * 3
            + [pltpu.VMEM((8, LANES), jnp.float32)],
            scratch_shapes=[
                pltpu.VMEM((count, 4, 2, 3, quarter, LANES), jnp.float32),
                pltpu.SemaphoreType.DMA((count, 4, 2)),
            ],
            compiler_params=pltpu.CompilerParams(vmem_limit_bytes=VMEM_ENCODE),
            name="encode",
        )(gx_place, *tables, *token)

    def first(c, own, given, before):
        count = sizes[c]
        fresh = before is None
        return pl.pallas_call(
            functools.partial(first_kernel, fresh),
            in_specs=[smem] * 3 + [vmem] * (4 if fresh else 5),
            out_specs=[vmem] * 5,
            out_shape=[POINTS, words(count, final, jnp.int32)] + [words(count, final)] * 3,
            scratch_shapes=work,
            input_output_aliases={} if fresh else {7: 0},
            compiler_params=small,
            name="first_rounds",
        )(challenges, gx_place, gy_place, own, *near(given), *(() if fresh else (before,)))

    def second(c, kept, given, before, folded):
        fresh, last = folded is None, c == chunks - 1
        shape = (3, polynomials, final, LANES)
        out_shape, out_specs = [POINTS] + [pltpu.VMEM(shape, jnp.float32)] * 2, [vmem] * 3
        scratch = list(work)
        if last:
            out_shape += [jax.ShapeDtypeStruct((devices, 1, LANES), jnp.float32)] + [jax.ShapeDtypeStruct(shape, jnp.float32)] * 2
            out_specs += [vmem, hbm, hbm]
            scratch.append(pltpu.SemaphoreType.DMA((2, 2)))
        return pl.pallas_call(
            functools.partial(second_kernel, starts[c], fresh, last),
            in_specs=[smem] * 3 + [vmem] * (5 if fresh else 7),
            out_specs=out_specs,
            out_shape=out_shape,
            scratch_shapes=scratch,
            input_output_aliases={7: 0} if fresh else {7: 0, 8: 1, 9: 2},
            compiler_params=small,
            name="second_rounds",
        )(challenges, gx_place, gy_place, kept, *near(given), before, *(() if fresh else folded))

    owns, sent = [], []
    token = []
    chunks = len(sizes)
    for c in range(chunks):
        own, *given, token = encode(c, token)
        token = [token]
        owns.append(own)
        sent.append([swap_with(x, "gx", (d + 1) << gx_shift) for d, x in enumerate(given)])
    points, folded, waiting = None, None, []
    for c in range(chunks + 1):
        if c < chunks:
            points, kept, *given = first(c, owns[c], sent[c], points)
            waiting.append((kept, [swap_with(x, "gy", (e + 1) << gy_shift) for e, x in enumerate(given)]))
        if c:
            points, *folded = second(c - 1, *waiting[c - 1], points, folded)
    sums, *folded = folded[2:]
    gathered = lax.all_to_all(sums, ("gx", "gy"), 0, 0)
    total = gathered.sum(axis=0).reshape(LANES)
    points = jnp.stack(settle(total[0:12], total[16:28], total[32:44])).reshape(3, 4, 3)
    shape = (3, polynomials, 1, 1, row_count // 16)
    return points, folded[0].reshape(shape), folded[1].reshape(shape)


def solution(mesh):
    tables = P(None, None, "gx", "gy", None)
    devices = mesh.shape["gx"] * mesh.shape["gy"]

    def body(*arrays):
        return shards(devices, *arrays)

    return jax.shard_map(
        body,
        mesh=mesh,
        in_specs=(tables, tables, P()),
        out_specs=(P(), tables, tables),
        check_vma=False,
    )
```

```python
import functools

import jax
import jax.numpy as jnp
from jax import lax
from jax.experimental import pallas as pl
from jax.experimental.pallas import tpu as pltpu
from jax.sharding import PartitionSpec as P


PRIME = 2147483647
LANES = 128
UNROLL = 4
VMEM_ENCODE, VMEM_KERNEL = 16 << 20, 8 << 20


def shr(x, n):
    return lax.shift_right_logical(x, jnp.int32(n))


def reduce_once(x):
    return (x & PRIME) + shr(x, 31)


def add_mod(a, b):
    return reduce_once(a + b)


def sub_mod(a, b):
    return reduce_once(a + (PRIME - b))


def limbs_of(v):
    return v & 2047, shr(v, 11) & 2047, shr(v, 22)


def word_of_limbs(l0, l1, l2):
    half = jnp.floor(l2 * 0.5)
    base = (l0 + l1 * 2048.0) + ((l2 - half * 2.0) * 4194304.0 + 8388608.0)
    negative = half >= 128.0
    scale = jnp.exp2(half - jnp.where(negative, 192.0, 64.0))
    return base * jnp.where(negative, -scale, scale)


def word_of_int(v):
    base = ((v & 8388607) + 8388608).astype(jnp.float32)
    negative = v >= 1073741824
    scale = jnp.exp2(((shr(v, 23) & 127) - 64).astype(jnp.float32))
    return base * jnp.where(negative, -scale, scale)


def int_of_word(x):
    size = jnp.abs(x)
    level = jnp.floor(jnp.log2(size) + 0.0009765625)
    value = size * jnp.exp2(23.0 - level)
    value = jnp.minimum(value, value + value - 8388608.0)
    offset = jnp.where(x < 0.0, jnp.int32((40 << 23) + (1 << 30)), jnp.int32(40 << 23))
    return value.astype(jnp.int32) + (level.astype(jnp.int32) << 23) + offset


def weighted_sum(limbs, weights):
    low = high = None
    for a, c in zip(limbs, weights):
        for n in range(3):
            low = a[n] * c[n] if low is None else low + a[n] * c[n]
            high = a[n] * c[3 + n] if high is None else high + a[n] * c[3 + n]
    return reduce_once(low + ((high & 32767) << 16) + shr(high, 15))


def degrees(a, b):
    return [
        a[0] * b[0],
        a[0] * b[1] + a[1] * b[0],
        a[0] * b[2] + a[1] * b[1] + a[2] * b[0],
        a[1] * b[2] + a[2] * b[1],
        a[2] * b[2],
    ]


def rotate(x, n):
    return ((x << n) & PRIME) + shr(x, 31 - n)


def element_of_degrees(d):
    total = add_mod(reduce_once(d[0]), rotate(d[1], 11))
    total = add_mod(total, rotate(d[2], 22))
    total = add_mod(total, rotate(d[3], 2))
    return add_mod(total, rotate(d[4], 13))


def mul_mod(a, b):
    return element_of_degrees(degrees(limbs_of(a), limbs_of(b)))


def add_limbs(a, b):
    return [x + y for x, y in zip(a, b)]


def nine_of(v):
    s02, s13 = add_limbs(v[0], v[2]), add_limbs(v[1], v[3])
    s01, s23 = add_limbs(v[0], v[1]), add_limbs(v[2], v[3])
    return [*v, s02, s13, s01, s23, add_limbs(s01, s23)]


MANY, ALL = range(8), range(9)


def clear(acc_ref, kinds):
    for kind in kinds:
        for n in range(5):
            acc_ref[5 * kind + n] = jnp.zeros((8, LANES), jnp.int32)


def two_rounds(acc_ref, splat_ref, s, w):
    s, w = [[x if isinstance(x, tuple) else limbs_of(x) for x in v] for v in (s, w)]
    for kind, (a, b) in enumerate(zip(nine_of(s), nine_of(w))):
        for n, d in enumerate(degrees(a, b)):
            acc_ref[5 * kind + n] = acc_ref[5 * kind + n] + d
    weights = [[splat_ref[6 * x + n] for n in range(6)] for x in range(4)]
    return weighted_sum(s, weights), weighted_sum(w, weights)


def flush(acc_ref, points_ref, first, kinds):
    for kind in kinds:
        here = element_of_degrees([acc_ref[5 * kind + n] for n in range(5)])
        points_ref[first + kind] = add_mod(points_ref[first + kind], here)


def over_pairs(count, tiles, accs, pair):
    assert tiles <= 16
    rare = [MANY if count * tiles <= 64 else () for _ in accs]

    def body(j, _):
        for (acc_ref, _, _), late in zip(accs, rare):
            clear(acc_ref, [k for k in ALL if k not in late])
        pair(j)
        for (acc_ref, points_ref, first), late in zip(accs, rare):
            flush(acc_ref, points_ref, first, [k for k in ALL if k not in late])

    for (acc_ref, _, _), late in zip(accs, rare):
        clear(acc_ref, late)
    lax.fori_loop(0, count, body, None)
    for (acc_ref, points_ref, first), late in zip(accs, rare):
        flush(acc_ref, points_ref, first, late)


def whole(scalar):
    return jnp.full((8, LANES), scalar, jnp.int32)


def sides(challenges_ref, place, phase):
    out = []
    for k in range(2):
        high = whole(challenges_ref[2 * phase + k])
        low = jnp.where(high == 0, 1, PRIME - high + 1)
        is_low = whole((place >> (1 - k)) & 1) == 0
        out.append((jnp.where(is_low, low, high), jnp.where(is_low, high, low)))
    return out


def constants_of(weight):
    parts = [weight, rotate(weight, 11), rotate(weight, 22)]
    return [x & 65535 for x in parts] + [shr(x, 16) for x in parts]


def splat_weights(challenges_ref, place, phase, splat_ref):
    first, second = sides(challenges_ref, place, phase)
    for x in range(4):
        for n, c in enumerate(constants_of(mul_mod(first[x >> 1], second[x & 1]))):
            splat_ref[6 * x + n] = c


def tile(start, i):
    return pl.ds(pl.multiple_of(start + i * 8, 8), 8)


def start_owns(owns, place, tables, outs, sems):
    copies = []
    for n, (start, count) in enumerate(owns):
        for t in range(2):
            out = outs[2 * n + t]
            rows = out.shape[2]
            src = tables[t].at[:, pl.ds(start, count), pl.ds(pl.multiple_of(place * rows, rows), rows), :]
            copies.append(pltpu.make_async_copy(src, out, sems.at[n, t]))
    for copy in copies:
        copy.start()
    return copies


def encode_kernel(raw, start, owns, gx_ref, gy_ref, s_hbm, w_hbm, *refs):
    if len(owns):
        refs, own_sems = refs[:-1], refs[-1]
    buffer, sems = refs[-2:]
    refs = refs[:-2]
    if len(owns):
        refs, own_outs = refs[: -2 * len(owns)], refs[-2 * len(owns) :]
    token_ref = refs[-1]
    outs = refs[-5:-1] if raw else refs[-4:-1]
    count, rows = buffer.shape[0], buffer.shape[4]
    shifts = (1, 2, 3, 0) if raw else (1, 2, 3)
    order = [(j, d, t) for j in range(count) for d in shifts for t in range(2)]

    def copy(j, d, t):
        src = (s_hbm, w_hbm)[t].at[:, start + j, pl.ds(pl.multiple_of((gx_ref[0] ^ d) * rows, rows), rows), :]
        return pltpu.make_async_copy(src, buffer.at[j, d % len(shifts), t], sems.at[j, d % len(shifts), t])

    for where in order:
        copy(*where).start()
    if len(owns):
        own_copies = start_owns(owns, gx_ref[0], (s_hbm, w_hbm), own_outs, own_sems)
    token_ref[...] = jnp.zeros_like(token_ref)
    sub = rows // 4
    for where in order:
        j, d, t = where
        slot = d % len(shifts)
        copy(*where).wait()
        for e in range(4 if raw else 1):
            first = (gy_ref[0] ^ e) * sub if raw else 0

            def step(i, _):
                word = word_of_limbs(*[buffer[j, slot, t, n, tile(first, i)] for n in range(3)])
                if raw:
                    outs[e][t, j, d, tile(0, i)] = word
                else:
                    outs[d - 1][t, j, tile(0, i)] = word

            lax.fori_loop(0, (sub if raw else rows) // 8, step, None, unroll=4)
    if len(owns):
        for copy_own in own_copies:
            copy_own.wait()


def gather_kernel(z0, z1, z2, z3, o1, o2, o3):
    for e, src in enumerate((z0, z1, z2, z3)):
        for d, out in enumerate((o1, o2, o3)):
            for t in range(2):
                for j in range(out.shape[1]):
                    out[t, j, e] = src[t, j, d + 1]


def first_kernel(fresh, challenges_ref, gx_ref, gy_ref, s_ref, w_ref, g1, g2, g3, *refs):
    if not fresh:
        before_ref, *refs = refs
    points_ref, kept_ref, o1, o2, o3, acc_ref, splat_ref = refs
    count, rows = s_ref.shape[1], s_ref.shape[2]
    sub = rows // 4
    given, outs = (g1, g2, g3), (kept_ref, o1, o2, o3)
    splat_weights(challenges_ref, gx_ref[0], 0, splat_ref)
    points_ref[...] = jnp.zeros_like(points_ref) if fresh else before_ref[...]

    def pair(j):
        for e in range(4):
            start = (gy_ref[0] ^ e) * sub

            def step(i, _):
                at = tile(start, i)
                values = []
                for t, own in enumerate((s_ref, w_ref)):
                    limbs = tuple(own[n, j, at].astype(jnp.int32) for n in range(3))
                    values.append([limbs] + [int_of_word(g[t, j, at]) for g in given])
                for t, folded in enumerate(two_rounds(acc_ref, splat_ref, *values)):
                    outs[e][t, j, tile(0, i)] = word_of_int(folded) if e else folded

            lax.fori_loop(0, sub // 8, step, None, unroll=UNROLL)

    over_pairs(count, rows // 8, [(acc_ref, points_ref, 0)], pair)


def settle(lowest, middle, highest, passes=3):
    for _ in range(passes):
        carried = jnp.floor(lowest * (1.0 / 2048.0))
        lowest = lowest - carried * 2048.0
        middle = middle + carried
        carried = jnp.floor(middle * (1.0 / 2048.0))
        middle = middle - carried * 2048.0
        highest = highest + carried
        carried = jnp.floor(highest * (1.0 / 512.0))
        highest = highest - carried * 512.0
        lowest = lowest + carried
    if passes < 3:
        return lowest, middle, highest
    at_modulus = (lowest == 2047.0) & (middle == 2047.0) & (highest == 511.0)
    return [jnp.where(at_modulus, 0.0, limb) for limb in (lowest, middle, highest)]


def round_sums(challenges_ref, place, phase, points):
    own, other = sides(challenges_ref, place, phase)[0]
    squares = [constants_of(mul_mod(*x)) for x in ((own, own), (own, other), (other, other))]
    i0, i1, i2, i3, i02, i13, i01, i23, i0123 = points
    first = [add_mod(i0, i1), add_mod(i2, i3), add_mod(i02, i13)]
    second = []
    for own, other, both in ((i0, i2, i02), (i1, i3, i13), (i01, i23, i0123)):
        cross = sub_mod(both, add_mod(own, other))
        second.append(weighted_sum([limbs_of(x) for x in (own, cross, other)], squares))
    return [first, second]


def publish_row(challenges_ref, places, points_ref, sums_ref):
    lane = lax.broadcasted_iota(jnp.int32, (1, LANES), 1)
    rows = [jnp.zeros((1, LANES), jnp.float32) for _ in range(3)]
    for phase in range(2):
        place = places[phase]
        points = [points_ref[9 * phase + n] for n in range(9)]
        for k, (own, other, both) in enumerate(round_sums(challenges_ref, place, phase, points)):
            is_low = whole((place >> (1 - k)) & 1) == 0
            at_zero = jnp.where(is_low, own, other)
            at_one = jnp.where(is_low, other, own)
            once = add_mod(at_zero, add_mod(at_one, at_one))
            at_two = sub_mod(add_mod(once, add_mod(once, once)), add_mod(both, both))
            for t, value in enumerate((at_zero, at_one, at_two)):
                for n, limb in enumerate(limbs_of(value)):
                    total = jnp.sum(limb.astype(jnp.float32), axis=(0, 1), keepdims=True)
                    rows[n] = jnp.where(lane == 6 * phase + 3 * k + t, total, rows[n])
    low, mid, high = settle(*rows, passes=1)
    packed = low + pltpu.roll(mid, 16, 1) + pltpu.roll(high, 32, 1)
    sums_ref[...] = jnp.broadcast_to(packed, sums_ref.shape)


class Finish:
    def __init__(self, early, late, s_ref, w_ref, refs):
        self.sums_ref, s_hbm, w_hbm, sems = refs
        self.parts = [
            [
                pltpu.make_async_copy(src.at[:, part], dst.at[:, part], sems.at[which, t])
                for t, (src, dst) in enumerate(((s_ref, s_hbm), (w_ref, w_hbm)))
            ]
            for which, part in enumerate((pl.ds(*early), pl.ds(*late)))
        ]
        self.start(0)

    def start(self, which):
        for copy in self.parts[which]:
            copy.start()

    def end(self, challenges_ref, places, points_ref):
        self.start(1)
        publish_row(challenges_ref, places, points_ref, self.sums_ref)
        for copy in self.parts[0] + self.parts[1]:
            copy.wait()


def put_folded(outs, j, at, folded):
    for out, value in zip(outs, folded):
        for n, limb in enumerate(limbs_of(jnp.where(value == PRIME, 0, value))):
            out[n, j, at] = limb.astype(jnp.float32)


def second_kernel(start, fresh, last, challenges_ref, gx_ref, gy_ref, kept_ref, g1, g2, g3, before_ref, *refs):
    if not fresh:
        refs = refs[2:]
    points_ref, s_ref, w_ref, *refs = refs
    count, rows = kept_ref.shape[1], kept_ref.shape[2]
    if last:
        finish = Finish((0, start), (start, count), s_ref, w_ref, refs[:3] + refs[5:])
        refs = refs[3:5]
    acc_ref, splat_ref = refs
    given = (g1, g2, g3)
    splat_weights(challenges_ref, gy_ref[0], 1, splat_ref)
    points_ref[...] = before_ref[...]

    def pair(j):
        def step(i, _):
            at = tile(0, i)
            s, w = [[kept_ref[t, j, at]] + [int_of_word(g[t, j, at]) for g in given] for t in range(2)]
            put_folded((s_ref, w_ref), start + j, at, two_rounds(acc_ref, splat_ref, s, w))

        lax.fori_loop(0, rows // 8, step, None, unroll=UNROLL)

    over_pairs(count, rows // 8, [(acc_ref, points_ref, 9)], pair)
    if last:
        finish.end(challenges_ref, (gx_ref[0], gy_ref[0]), points_ref)


def all_kernel(start, fresh, last, challenges_ref, gx_ref, gy_ref, z0, z1, z2, z3, g1, g2, g3, before_ref, *refs):
    if not fresh:
        refs = refs[2:]
    points_ref, s_ref, w_ref, *refs = refs
    count, rows = z0.shape[1], z0.shape[3]
    if last:
        finish = Finish((0, start), (start, count), s_ref, w_ref, refs[:3] + refs[5 + 3 :])
        refs = refs[3 : 5 + 3]
    acc_ref, splat_ref, acc2_ref, splat2_ref, once = refs
    given = (g1, g2, g3)
    splat_weights(challenges_ref, gx_ref[0], 0, splat_ref)
    splat_weights(challenges_ref, gy_ref[0], 1, splat2_ref)
    points_ref[...] = before_ref[...]

    def pair(j):
        for e, own in enumerate((z0, z1, z2, z3)):

            def step(i, _):
                at = tile(0, i)
                s, w = [[int_of_word(x) for x in [own[t, j, 0, at]] + [g[t, j, e, at] for g in given]] for t in range(2)]
                for t, folded in enumerate(two_rounds(acc_ref, splat_ref, s, w)):
                    once[t, e, at] = folded

            lax.fori_loop(0, rows // 8, step, None, unroll=UNROLL)

        def step(i, _):
            at = tile(0, i)
            s, w = [[once[t, e, at] for e in range(4)] for t in range(2)]
            put_folded((s_ref, w_ref), start + j, at, two_rounds(acc2_ref, splat2_ref, s, w))

        lax.fori_loop(0, rows // 8, step, None, unroll=UNROLL)

    over_pairs(count, rows // 2, [(acc_ref, points_ref, 0), (acc2_ref, points_ref, 9)], pair)
    if last:
        finish.end(challenges_ref, (gx_ref[0], gy_ref[0]), points_ref)


def swap_with(x, axis, mask):
    return lax.ppermute(x, axis, [(i, i ^ mask) for i in range(lax.axis_size(axis))])


CHUNKS, RAW = (3, 3), 2
SENDS = "0R1"
STEPS = ("A0", "G", "A1", "B0", "K", "B1")
POINTS = pltpu.VMEM((18, 8, LANES), jnp.int32)


def plan(polynomials):
    if sum(CHUNKS) + RAW == polynomials:
        return CHUNKS, RAW, SENDS, STEPS
    sizes = (1,) * polynomials
    steps = ["A0"] + [x for c in range(1, polynomials) for x in (f"A{c}", f"B{c - 1}")] + [f"B{polynomials - 1}"]
    return sizes, 0, range(polynomials), steps


def shards(devices, selectors, proofs, challenges):
    polynomials, row_count = selectors.shape[1], selectors.shape[-1]
    lane_rows = row_count // LANES
    quarter, final = lane_rows // 4, lane_rows // 16
    tables = [
        pltpu.with_memory_space_constraint(x.reshape(3, polynomials, lane_rows, LANES), pltpu.HBM)
        for x in (selectors, proofs)
    ]
    gx_shift = lax.axis_size("gx").bit_length() - 3
    gy_shift = lax.axis_size("gy").bit_length() - 3
    gx_place = (lax.axis_index("gx") >> gx_shift).astype(jnp.int32).reshape(1)
    gy_place = (lax.axis_index("gy") >> gy_shift).astype(jnp.int32).reshape(1)

    sizes, raw, sends, steps = plan(polynomials)
    raw_last = steps[-1] == "K"
    raw_start = polynomials - raw if raw_last else 0
    starts = [sum(sizes[:c]) + (0 if raw_last else raw) for c in range(len(sizes))]
    smem, vmem, hbm, anywhere = [pl.BlockSpec(memory_space=m) for m in (pltpu.SMEM, pltpu.VMEM, pltpu.HBM, pl.ANY)]

    def words(count, rows, dtype=jnp.float32):
        return pltpu.VMEM((2, count, *rows, LANES), dtype)

    def near(arrays):
        return [pltpu.with_memory_space_constraint(x, pltpu.VMEM) for x in arrays]

    work = [pltpu.VMEM((45, 8, LANES), jnp.int32), pltpu.VMEM((24, 8, LANES), jnp.int32)]
    small = pltpu.CompilerParams(vmem_limit_bytes=VMEM_KERNEL)

    def encode(raw_chunk, start, count, outs, owns, token):
        out_shape = outs + [pltpu.VMEM((8, LANES), jnp.float32)]
        out_shape += [pltpu.VMEM((3, n, quarter, LANES), jnp.float32) for _, n in owns for _ in range(2)]
        shifts = 4 if raw_chunk else 3
        scratch = [
            pltpu.VMEM((count, shifts, 2, 3, quarter, LANES), jnp.float32),
            pltpu.SemaphoreType.DMA((count, shifts, 2)),
        ]
        if owns:
            scratch.append(pltpu.SemaphoreType.DMA((len(owns), 2)))
        return pl.pallas_call(
            functools.partial(encode_kernel, raw_chunk, start, owns),
            in_specs=[smem, smem, hbm, hbm] + [anywhere] * len(token),
            out_specs=[vmem] * len(out_shape),
            out_shape=out_shape,
            scratch_shapes=scratch,
            compiler_params=pltpu.CompilerParams(vmem_limit_bytes=VMEM_ENCODE),
            name="encode",
        )(gx_place, gy_place, *tables, *token)

    def first(c, own, given, before):
        count = sizes[c]
        fresh = before is None
        return pl.pallas_call(
            functools.partial(first_kernel, fresh),
            in_specs=[smem] * 3 + [vmem] * (5 if fresh else 6),
            out_specs=[vmem] * 5,
            out_shape=[POINTS, words(count, [final], jnp.int32)] + [words(count, [final])] * 3,
            scratch_shapes=work,
            input_output_aliases={} if fresh else {8: 0},
            compiler_params=small,
            name="first_rounds",
        )(challenges, gx_place, gy_place, *own, *near(given), *(() if fresh else (before,)))

    def fold_last(kernel, start, arrays, before, folded, last, scratch):
        fresh = folded is None
        shape = (3, polynomials, final, LANES)
        out_shape, out_specs = [POINTS] + [pltpu.VMEM(shape, jnp.float32)] * 2, [vmem] * 3
        if last:
            out_shape += [jax.ShapeDtypeStruct((devices, 1, LANES), jnp.float32)] + [jax.ShapeDtypeStruct(shape, jnp.float32)] * 2
            out_specs += [vmem, hbm, hbm]
            scratch = scratch + [pltpu.SemaphoreType.DMA((2, 2))]
        at = 3 + len(arrays)
        return pl.pallas_call(
            functools.partial(kernel, start, fresh, last),
            in_specs=[smem] * 3 + [vmem] * (len(arrays) + (1 if fresh else 3)),
            out_specs=out_specs,
            out_shape=out_shape,
            scratch_shapes=scratch,
            input_output_aliases={at: 0} if fresh else {at: 0, at + 1: 1, at + 2: 2},
            compiler_params=small,
        )(challenges, gx_place, gy_place, *near(arrays), before, *(() if fresh else folded))

    def swap(arrays, axis, shift):
        return [swap_with(x, axis, (d + 1) << shift) for d, x in enumerate(arrays)]

    owns, sent, token = {}, {}, []
    reader = list(sends)[min(1, len(sends) - 1)]
    ranges = list(zip(starts, sizes))
    for c in sends:
        raw_chunk = c == "R"
        if raw_chunk:
            start, count, outs = raw_start, raw, [words(raw, [4, final])] * 4
        else:
            start, count = ranges[int(c)]
            outs = [words(count, [quarter])] * 3
        out = encode(raw_chunk, start, count, outs, ranges if c == reader else [], token)
        given, token = out[: len(outs)], [out[len(outs)]]
        if raw_chunk:
            raw_own, *given = given
        if c == reader:
            rest = out[len(outs) + 1 :]
            owns = {n: rest[2 * n : 2 * n + 2] for n in range(len(ranges))}
        sent[c if raw_chunk else int(c)] = swap(given, *(("gy", gy_shift) if raw_chunk else ("gx", gx_shift)))
    points, folded, waiting = None, None, {}
    for step in steps:
        last = step == steps[-1]
        c = int(step[1:] or 0)
        if step[0] == "A":
            points, kept, *given = first(c, owns[c], sent[c], points)
        elif step[0] == "G":
            around = [raw_own, *sent["R"]]
            given = pl.pallas_call(
                gather_kernel,
                in_specs=[vmem] * 4,
                out_specs=[vmem] * 3,
                out_shape=[words(raw, [4, final])] * 3,
                compiler_params=small,
                name="gather",
            )(*near(around))
        elif step[0] == "K":
            scratch = work + work + [pltpu.VMEM((2, 4, final, LANES), jnp.int32)]
            points, *folded = fold_last(all_kernel, raw_start, around + given_raw, points, folded, last, scratch)
        else:
            points, *folded = fold_last(second_kernel, starts[c], waiting[c], points, folded, last, work)
        if step[0] == "A":
            waiting[c] = [kept, *swap(given, "gy", gy_shift)]
        elif step[0] == "G":
            given_raw = swap(given, "gx", gx_shift)
    sums, *folded = folded[2:]
    gathered = lax.all_to_all(sums, ("gx", "gy"), 0, 0)
    total = gathered.sum(axis=0).reshape(LANES)
    points = jnp.stack(settle(total[0:12], total[16:28], total[32:44])).reshape(3, 4, 3)
    shape = (3, polynomials, 1, 1, row_count // 16)
    return points, folded[0].reshape(shape), folded[1].reshape(shape)


def solution(mesh):
    tables = P(None, None, "gx", "gy", None)
    devices = mesh.shape["gx"] * mesh.shape["gy"]

    def body(*arrays):
        return shards(devices, *arrays)

    return jax.shard_map(
        body,
        mesh=mesh,
        in_specs=(tables, tables, P()),
        out_specs=(P(), tables, tables),
        check_vma=False,
    )
```

```python
import functools

import jax
import jax.numpy as jnp
from jax import lax
from jax.experimental import pallas as pl
from jax.experimental.pallas import tpu as pltpu
from jax.sharding import PartitionSpec as P


PRIME = 2147483647
LANES = 128
UNROLL = 4
VMEM_ENCODE, VMEM_KERNEL = 16 << 20, 8 << 20


def shr(x, n):
    return lax.shift_right_logical(x, jnp.int32(n))


def reduce_once(x):
    return (x & PRIME) + shr(x, 31)


def add_mod(a, b):
    return reduce_once(a + b)


def sub_mod(a, b):
    return reduce_once(a + (PRIME - b))


def limbs_of(v):
    return v & 2047, shr(v, 11) & 2047, shr(v, 22)


def word_of_limbs(l0, l1, l2):
    half = jnp.floor(l2 * 0.5)
    base = (l0 + l1 * 2048.0) + ((l2 - half * 2.0) * 4194304.0 + 8388608.0)
    negative = half >= 128.0
    scale = jnp.exp2(half - jnp.where(negative, 192.0, 64.0))
    return base * jnp.where(negative, -scale, scale)


def word_of_int(v):
    base = ((v & 8388607) + 8388608).astype(jnp.float32)
    negative = v >= 1073741824
    scale = jnp.exp2(((shr(v, 23) & 127) - 64).astype(jnp.float32))
    return base * jnp.where(negative, -scale, scale)


def int_of_word(x):
    size = jnp.abs(x)
    level = jnp.floor(jnp.log2(size) + 0.0009765625)
    value = size * jnp.exp2(23.0 - level)
    value = jnp.minimum(value, value + value - 8388608.0)
    offset = jnp.where(x < 0.0, jnp.int32((40 << 23) + (1 << 30)), jnp.int32(40 << 23))
    return value.astype(jnp.int32) + (level.astype(jnp.int32) << 23) + offset


def weighted_sum(limbs, weights):
    low = high = None
    for a, c in zip(limbs, weights):
        for n in range(3):
            low = a[n] * c[n] if low is None else low + a[n] * c[n]
            high = a[n] * c[3 + n] if high is None else high + a[n] * c[3 + n]
    return reduce_once(low + ((high & 32767) << 16) + shr(high, 15))


def degrees(a, b):
    return [
        a[0] * b[0],
        a[0] * b[1] + a[1] * b[0],
        a[0] * b[2] + a[1] * b[1] + a[2] * b[0],
        a[1] * b[2] + a[2] * b[1],
        a[2] * b[2],
    ]


def rotate(x, n):
    return ((x << n) & PRIME) + shr(x, 31 - n)


def element_of_degrees(d):
    total = add_mod(reduce_once(d[0]), rotate(d[1], 11))
    total = add_mod(total, rotate(d[2], 22))
    total = add_mod(total, rotate(d[3], 2))
    return add_mod(total, rotate(d[4], 13))


def mul_mod(a, b):
    return element_of_degrees(degrees(limbs_of(a), limbs_of(b)))


def add_limbs(a, b):
    return [x + y for x, y in zip(a, b)]


def nine_of(v):
    s02, s13 = add_limbs(v[0], v[2]), add_limbs(v[1], v[3])
    s01, s23 = add_limbs(v[0], v[1]), add_limbs(v[2], v[3])
    return [*v, s02, s13, s01, s23, add_limbs(s01, s23)]


MANY, ALL = range(8), range(9)


def clear(acc_ref, kinds):
    for kind in kinds:
        for n in range(5):
            acc_ref[5 * kind + n] = jnp.zeros((8, LANES), jnp.int32)


def two_rounds(acc_ref, weights_ref, phase, s, w):
    s, w = [[x if isinstance(x, tuple) else limbs_of(x) for x in v] for v in (s, w)]
    for kind, (a, b) in enumerate(zip(nine_of(s), nine_of(w))):
        for n, d in enumerate(degrees(a, b)):
            acc_ref[5 * kind + n] = acc_ref[5 * kind + n] + d
    weights = [[weights_ref[24 * phase + 6 * x + n] for n in range(6)] for x in range(4)]
    return weighted_sum(s, weights), weighted_sum(w, weights)


def flush(acc_ref, points_ref, first, kinds):
    for kind in kinds:
        here = element_of_degrees([acc_ref[5 * kind + n] for n in range(5)])
        points_ref[first + kind] = add_mod(points_ref[first + kind], here)


def over_pairs(count, tiles, accs, pair):
    assert tiles <= 16
    rare = [MANY if count * tiles <= 64 else () for _ in accs]

    def body(j, _):
        for (acc_ref, _, _), late in zip(accs, rare):
            clear(acc_ref, [k for k in ALL if k not in late])
        pair(j)
        for (acc_ref, points_ref, first), late in zip(accs, rare):
            flush(acc_ref, points_ref, first, [k for k in ALL if k not in late])

    for (acc_ref, _, _), late in zip(accs, rare):
        clear(acc_ref, late)
    lax.fori_loop(0, count, body, None)
    for (acc_ref, points_ref, first), late in zip(accs, rare):
        flush(acc_ref, points_ref, first, late)


def whole(scalar):
    return jnp.full((8, LANES), scalar, jnp.int32)


def sides(challenges_ref, place, phase):
    out = []
    for k in range(2):
        high = whole(challenges_ref[2 * phase + k])
        low = jnp.where(high == 0, 1, PRIME - high + 1)
        is_low = whole((place >> (1 - k)) & 1) == 0
        out.append((jnp.where(is_low, low, high), jnp.where(is_low, high, low)))
    return out


def constants_of(weight):
    parts = [weight, rotate(weight, 11), rotate(weight, 22)]
    return [x & 65535 for x in parts] + [shr(x, 16) for x in parts]


SQUARES, LOW_SIDE, WEIGHTS = 48, 84, 88


def place_of(axis):
    return lax.axis_index(axis) >> (lax.axis_size(axis).bit_length() - 3)


def weights_kernel(challenges_ref, weights_ref):
    for phase, axis in enumerate(("gx", "gy")):
        place = place_of(axis)
        first, second = sides(challenges_ref, place, phase)
        for x in range(4):
            for n, c in enumerate(constants_of(mul_mod(first[x >> 1], second[x & 1]))):
                weights_ref[24 * phase + 6 * x + n] = c
        own, other = first
        for x, pair in enumerate(((own, own), (own, other), (other, other))):
            for n, c in enumerate(constants_of(mul_mod(*pair))):
                weights_ref[SQUARES + 18 * phase + 6 * x + n] = c
        for k in range(2):
            weights_ref[LOW_SIDE + 2 * phase + k] = whole((place >> (1 - k)) & 1)


def tile(start, i):
    return pl.ds(pl.multiple_of(start + i * 8, 8), 8)


def over_tiles(rows, step):
    lax.fori_loop(0, rows // 8, step, None, unroll=min(UNROLL, rows // 8))


def item_of(table, item, quarter):
    parts = table.shape[4]
    return table.at[:, item // parts, quarter, :, item % parts]


def encode_kernel(raw, start, owns, s_hbm, w_hbm, *refs):
    tables = (s_hbm, w_hbm)
    gx, gy = place_of("gx"), place_of("gy")
    own_copies = []
    if len(owns):
        refs, own_sems = refs[:-1], refs[-1]
    buffer, sems = refs[-2:]
    refs = refs[:-2]
    if len(owns):
        refs, own_outs = refs[: -2 * len(owns)], refs[-2 * len(owns) :]
        own_copies = [
            pltpu.make_async_copy(item_of(tables[t], first + i, gx), own_outs[2 * n + t].at[:, i], own_sems.at[n, i, t])
            for n, (first, count) in enumerate(owns)
            for i in range(count)
            for t in range(2)
        ]
    token_ref = refs[-1]
    outs = refs[-5:-1] if raw else refs[-4:-1]
    count, rows = buffer.shape[0], buffer.shape[5]
    shifts = (1, 2, 3, 0) if raw else (1, 2, 3)
    order = [(i, d, t) for i in range(count) for d in shifts for t in range(2)]

    def copy(i, d, t):
        slot = d % len(shifts)
        return pltpu.make_async_copy(item_of(tables[t], start + i, gx ^ d), buffer.at[i, slot, t], sems.at[i, slot, t])

    for where in order:
        copy(*where).start()
    for copy_own in own_copies:
        copy_own.start()
    token_ref[...] = jnp.zeros_like(token_ref)
    for where in order:
        i, d, t = where
        copy(*where).wait()
        for e in range(4):
            src = gy ^ e if raw else e
            for k in range(rows // 8):
                at = pl.ds(8 * k, 8)
                word = word_of_limbs(*[buffer[i, d % len(shifts), t, n, src, at] for n in range(3)])
                if raw:
                    outs[e][t, i, d, at] = word
                else:
                    outs[d - 1][t, i, e, at] = word
    for copy_own in own_copies:
        copy_own.wait()


def gather_kernel(z0, z1, z2, z3, o1, o2, o3):
    for e, src in enumerate((z0, z1, z2, z3)):
        for d, out in enumerate((o1, o2, o3)):
            for t in range(2):
                for j in range(out.shape[1]):
                    out[t, j, e] = src[t, j, d + 1]


def first_kernel(fresh, weights_ref, s_ref, w_ref, g1, g2, g3, *refs):
    if not fresh:
        before_ref, *refs = refs
    points_ref, kept_ref, o1, o2, o3, acc_ref = refs
    count, rows = s_ref.shape[1], s_ref.shape[3]
    given, outs = (g1, g2, g3), (kept_ref, o1, o2, o3)
    gy = place_of("gy")
    points_ref[...] = jnp.zeros_like(points_ref) if fresh else before_ref[...]

    def pair(j):
        for e in range(4):
            src = gy ^ e

            def step(i, _):
                at = tile(0, i)
                values = []
                for t, own in enumerate((s_ref, w_ref)):
                    limbs = tuple(own[n, j, src, at].astype(jnp.int32) for n in range(3))
                    values.append([limbs] + [int_of_word(g[t, j, src, at]) for g in given])
                for t, folded in enumerate(two_rounds(acc_ref, weights_ref, 0, *values)):
                    outs[e][t, j, at] = word_of_int(folded) if e else folded

            over_tiles(rows, step)

    over_pairs(count, rows // 2, [(acc_ref, points_ref, 0)], pair)


def settle(lowest, middle, highest, passes=3):
    for _ in range(passes):
        carried = jnp.floor(lowest * (1.0 / 2048.0))
        lowest = lowest - carried * 2048.0
        middle = middle + carried
        carried = jnp.floor(middle * (1.0 / 2048.0))
        middle = middle - carried * 2048.0
        highest = highest + carried
        carried = jnp.floor(highest * (1.0 / 512.0))
        highest = highest - carried * 512.0
        lowest = lowest + carried
    if passes < 3:
        return lowest, middle, highest
    at_modulus = (lowest == 2047.0) & (middle == 2047.0) & (highest == 511.0)
    return [jnp.where(at_modulus, 0.0, limb) for limb in (lowest, middle, highest)]


def round_sums(weights_ref, phase, points):
    squares = [[weights_ref[SQUARES + 18 * phase + 6 * x + n] for n in range(6)] for x in range(3)]
    i0, i1, i2, i3, i02, i13, i01, i23, i0123 = points
    first = [add_mod(i0, i1), add_mod(i2, i3), add_mod(i02, i13)]
    second = []
    for own, other, both in ((i0, i2, i02), (i1, i3, i13), (i01, i23, i0123)):
        cross = sub_mod(both, add_mod(own, other))
        second.append(weighted_sum([limbs_of(x) for x in (own, cross, other)], squares))
    return [first, second]


def publish_row(weights_ref, points_ref, sums_ref):
    lane = lax.broadcasted_iota(jnp.int32, (1, LANES), 1)
    rows = [jnp.zeros((1, LANES), jnp.float32) for _ in range(3)]
    for phase in range(2):
        points = [points_ref[9 * phase + n] for n in range(9)]
        for k, (own, other, both) in enumerate(round_sums(weights_ref, phase, points)):
            is_low = weights_ref[LOW_SIDE + 2 * phase + k] == 0
            at_zero = jnp.where(is_low, own, other)
            at_one = jnp.where(is_low, other, own)
            once = add_mod(at_zero, add_mod(at_one, at_one))
            at_two = sub_mod(add_mod(once, add_mod(once, once)), add_mod(both, both))
            for t, value in enumerate((at_zero, at_one, at_two)):
                for n, limb in enumerate(limbs_of(value)):
                    total = jnp.sum(limb.astype(jnp.float32), axis=(0, 1), keepdims=True)
                    rows[n] = jnp.where(lane == 6 * phase + 3 * k + t, total, rows[n])
    low, mid, high = settle(*rows, passes=1)
    packed = low + pltpu.roll(mid, 16, 1) + pltpu.roll(high, 32, 1)
    sums_ref[...] = jnp.broadcast_to(packed, sums_ref.shape)


class Finish:
    def __init__(self, early, late, s_ref, w_ref, refs):
        self.sums_ref, s_hbm, w_hbm, sems = refs
        self.parts = [
            [
                pltpu.make_async_copy(src.at[:, part], dst.at[:, part], sems.at[which, t])
                for t, (src, dst) in enumerate(((s_ref, s_hbm), (w_ref, w_hbm)))
            ]
            for which, part in enumerate((pl.ds(*early), pl.ds(*late)))
        ]
        self.start(0)

    def start(self, which):
        for copy in self.parts[which]:
            copy.start()

    def end(self, weights_ref, points_ref):
        self.start(1)
        publish_row(weights_ref, points_ref, self.sums_ref)
        for copy in self.parts[0] + self.parts[1]:
            copy.wait()


def put_folded(outs, j, at, folded):
    for out, value in zip(outs, folded):
        for n, limb in enumerate(limbs_of(jnp.where(value == PRIME, 0, value))):
            out[n, j, at] = limb.astype(jnp.float32)


def second_kernel(start, fresh, last, weights_ref, kept_ref, g1, g2, g3, before_ref, *refs):
    if not fresh:
        refs = refs[2:]
    points_ref, s_ref, w_ref, *refs = refs
    count, rows = kept_ref.shape[1], kept_ref.shape[2]
    if last:
        finish = Finish((0, start), (start, count), s_ref, w_ref, refs[:3] + refs[4:])
        refs = refs[3:4]
    (acc_ref,) = refs
    given = (g1, g2, g3)
    points_ref[...] = before_ref[...]

    def pair(j):
        def step(i, _):
            at = tile(0, i)
            s, w = [[kept_ref[t, j, at]] + [int_of_word(g[t, j, at]) for g in given] for t in range(2)]
            put_folded((s_ref, w_ref), start + j, at, two_rounds(acc_ref, weights_ref, 1, s, w))

        over_tiles(rows, step)

    over_pairs(count, rows // 8, [(acc_ref, points_ref, 9)], pair)
    if last:
        finish.end(weights_ref, points_ref)


def all_kernel(start, fresh, last, weights_ref, z0, z1, z2, z3, g1, g2, g3, before_ref, *refs):
    if not fresh:
        refs = refs[2:]
    points_ref, s_ref, w_ref, *refs = refs
    count, rows = z0.shape[1], z0.shape[3]
    if last:
        finish = Finish((0, start), (start, count), s_ref, w_ref, refs[:3] + refs[6:])
        refs = refs[3:6]
    acc_ref, acc2_ref, once = refs
    given = (g1, g2, g3)
    points_ref[...] = before_ref[...]

    def pair(j):
        for e, own in enumerate((z0, z1, z2, z3)):

            def step(i, _):
                at = tile(0, i)
                s, w = [[int_of_word(x) for x in [own[t, j, 0, at]] + [g[t, j, e, at] for g in given]] for t in range(2)]
                for t, folded in enumerate(two_rounds(acc_ref, weights_ref, 0, s, w)):
                    once[t, e, at] = folded

            over_tiles(rows, step)

        def step(i, _):
            at = tile(0, i)
            s, w = [[once[t, e, at] for e in range(4)] for t in range(2)]
            put_folded((s_ref, w_ref), start + j, at, two_rounds(acc2_ref, weights_ref, 1, s, w))

        over_tiles(rows, step)

    over_pairs(count, rows // 2, [(acc_ref, points_ref, 0), (acc2_ref, points_ref, 9)], pair)
    if last:
        finish.end(weights_ref, points_ref)


def swap_with(x, axis, mask):
    return lax.ppermute(x, axis, [(i, i ^ mask) for i in range(lax.axis_size(axis))])


SPLIT = 1
CHUNKS, RAW = (4, 2), 2
SENDS = "0R1"
STEPS = ("A0", "G", "A1", "B0", "K", "B1")
POINTS = pltpu.VMEM((18, 8, LANES), jnp.int32)


def plan(items):
    if sum(CHUNKS) + RAW == items:
        return CHUNKS, RAW, SENDS, STEPS
    steps = ["A0"] + [x for c in range(1, items) for x in (f"A{c}", f"B{c - 1}")] + [f"B{items - 1}"]
    return (1,) * items, 0, range(items), steps


def shards(devices, selectors, proofs, challenges):
    polynomials, row_count = selectors.shape[1], selectors.shape[-1]
    lane_rows = row_count // LANES
    parts = SPLIT if lane_rows % (128 * SPLIT) == 0 else 1
    items, final = polynomials * parts, lane_rows // 16 // parts
    shape = (3, polynomials, 4, 4, parts, final, LANES)
    tables = [pltpu.with_memory_space_constraint(x.reshape(shape), pltpu.HBM) for x in (selectors, proofs)]
    gx_shift = lax.axis_size("gx").bit_length() - 3
    gy_shift = lax.axis_size("gy").bit_length() - 3

    sizes, raw, sends, steps = plan(items)
    raw_last = steps[-1] == "K"
    raw_start = items - raw if raw_last else 0
    starts = [sum(sizes[:c]) + (0 if raw_last else raw) for c in range(len(sizes))]
    smem, vmem, hbm, anywhere = [pl.BlockSpec(memory_space=m) for m in (pltpu.SMEM, pltpu.VMEM, pltpu.HBM, pl.ANY)]

    def words(count, rows, dtype=jnp.float32):
        return pltpu.VMEM((2, count, *rows, LANES), dtype)

    def near(arrays):
        return [pltpu.with_memory_space_constraint(x, pltpu.VMEM) for x in arrays]

    work = [pltpu.VMEM((45, 8, LANES), jnp.int32)]
    small = pltpu.CompilerParams(vmem_limit_bytes=VMEM_KERNEL)

    def encode(raw_chunk, start, count, outs, owns, token):
        out_shape = outs + [pltpu.VMEM((8, LANES), jnp.float32)]
        out_shape += [pltpu.VMEM((3, n, 4, final, LANES), jnp.float32) for _, n in owns for _ in range(2)]
        shifts = 4 if raw_chunk else 3
        scratch = [
            pltpu.VMEM((count, shifts, 2, 3, 4, final, LANES), jnp.float32),
            pltpu.SemaphoreType.DMA((count, shifts, 2)),
        ]
        if owns:
            scratch.append(pltpu.SemaphoreType.DMA((len(owns), max(n for _, n in owns), 2)))
        return pl.pallas_call(
            functools.partial(encode_kernel, raw_chunk, start, owns),
            in_specs=[hbm, hbm] + [anywhere] * len(token),
            out_specs=[vmem] * len(out_shape),
            out_shape=out_shape,
            scratch_shapes=scratch,
            compiler_params=pltpu.CompilerParams(vmem_limit_bytes=VMEM_ENCODE),
            name="encode",
        )(*tables, *token)

    def first(c, own, given, before):
        count = sizes[c]
        fresh = before is None
        return pl.pallas_call(
            functools.partial(first_kernel, fresh),
            in_specs=[vmem] * (6 if fresh else 7),
            out_specs=[vmem] * 5,
            out_shape=[POINTS, words(count, [final], jnp.int32)] + [words(count, [final])] * 3,
            scratch_shapes=work,
            input_output_aliases={} if fresh else {6: 0},
            compiler_params=small,
            name="first_rounds",
        )(weights, *own, *near(given), *(() if fresh else (before,)))

    def fold_last(kernel, start, arrays, before, folded, last, scratch):
        fresh = folded is None
        shape = (3, items, final, LANES)
        out_shape, out_specs = [POINTS] + [pltpu.VMEM(shape, jnp.float32)] * 2, [vmem] * 3
        if last:
            out_shape += [jax.ShapeDtypeStruct((devices, 1, LANES), jnp.float32)] + [jax.ShapeDtypeStruct(shape, jnp.float32)] * 2
            out_specs += [vmem, hbm, hbm]
            scratch = scratch + [pltpu.SemaphoreType.DMA((2, 2))]
        at = 1 + len(arrays)
        return pl.pallas_call(
            functools.partial(kernel, start, fresh, last),
            in_specs=[vmem] * (len(arrays) + (2 if fresh else 4)),
            out_specs=out_specs,
            out_shape=out_shape,
            scratch_shapes=scratch,
            input_output_aliases={at: 0} if fresh else {at: 0, at + 1: 1, at + 2: 2},
            compiler_params=small,
        )(weights, *near(arrays), before, *(() if fresh else folded))

    def swap(arrays, axis, shift):
        return [swap_with(x, axis, (d + 1) << shift) for d, x in enumerate(arrays)]

    owns, sent, token = {}, {}, []
    reader = list(sends)[min(1, len(sends) - 1)]
    ranges = list(zip(starts, sizes))
    for c in sends:
        raw_chunk = c == "R"
        if raw_chunk:
            start, count, outs = raw_start, raw, [words(raw, [4, final])] * 4
        else:
            start, count = ranges[int(c)]
            outs = [words(count, [4, final])] * 3
        out = encode(raw_chunk, start, count, outs, ranges if c == reader else [], token)
        given, token = out[: len(outs)], [out[len(outs)]]
        if raw_chunk:
            raw_own, *given = given
        if c == reader:
            rest = out[len(outs) + 1 :]
            owns = {n: rest[2 * n : 2 * n + 2] for n in range(len(ranges))}
        sent[c if raw_chunk else int(c)] = swap(given, *(("gy", gy_shift) if raw_chunk else ("gx", gx_shift)))
    weights = pl.pallas_call(
        weights_kernel,
        in_specs=[smem],
        out_specs=vmem,
        out_shape=pltpu.VMEM((WEIGHTS, 8, LANES), jnp.int32),
        compiler_params=small,
        name="weights",
    )(challenges)
    points, folded, waiting = None, None, {}
    for step in steps:
        last = step == steps[-1]
        c = int(step[1:] or 0)
        if step[0] == "A":
            points, kept, *given = first(c, owns[c], sent[c], points)
        elif step[0] == "G":
            around = [raw_own, *sent["R"]]
            given = pl.pallas_call(
                gather_kernel,
                in_specs=[vmem] * 4,
                out_specs=[vmem] * 3,
                out_shape=[words(raw, [4, final])] * 3,
                compiler_params=small,
                name="gather",
            )(*near(around))
        elif step[0] == "K":
            scratch = work + work + [pltpu.VMEM((2, 4, final, LANES), jnp.int32)]
            points, *folded = fold_last(all_kernel, raw_start, around + given_raw, points, folded, last, scratch)
        else:
            points, *folded = fold_last(second_kernel, starts[c], waiting[c], points, folded, last, work)
        if step[0] == "A":
            waiting[c] = [kept, *swap(given, "gy", gy_shift)]
        elif step[0] == "G":
            given_raw = swap(given, "gx", gx_shift)
    sums, *folded = folded[2:]
    gathered = lax.all_to_all(sums, ("gx", "gy"), 0, 0)
    total = gathered.sum(axis=0).reshape(LANES)
    points = jnp.stack(settle(total[0:12], total[16:28], total[32:44])).reshape(3, 4, 3)
    shape = (3, polynomials, 1, 1, row_count // 16)
    return points, folded[0].reshape(shape), folded[1].reshape(shape)


def solution(mesh):
    tables = P(None, None, "gx", "gy", None)
    devices = mesh.shape["gx"] * mesh.shape["gy"]

    def body(*arrays):
        return shards(devices, *arrays)

    return jax.shard_map(
        body,
        mesh=mesh,
        in_specs=(tables, tables, P()),
        out_specs=(P(), tables, tables),
        check_vma=False,
    )
```

```python
import functools

import jax
import jax.numpy as jnp
from jax import lax
from jax.experimental import pallas as pl
from jax.experimental.pallas import tpu as pltpu
from jax.sharding import PartitionSpec as P


PRIME = 2147483647
LANES = 128
UNROLL = 4
VMEM_ENCODE, VMEM_KERNEL = 16 << 20, 8 << 20


def shr(x, n):
    return lax.shift_right_logical(x, jnp.int32(n))


def reduce_once(x):
    return (x & PRIME) + shr(x, 31)


def add_mod(a, b):
    return reduce_once(a + b)


def sub_mod(a, b):
    return reduce_once(a + (PRIME - b))


def limbs_of(v):
    return v & 2047, shr(v, 11) & 2047, shr(v, 22)


def word_of_limbs(l0, l1, l2):
    half = jnp.floor(l2 * 0.5)
    base = (l0 + l1 * 2048.0) + ((l2 - half * 2.0) * 4194304.0 + 8388608.0)
    negative = half >= 128.0
    scale = jnp.exp2(half - jnp.where(negative, 192.0, 64.0))
    return base * jnp.where(negative, -scale, scale)


def word_of_int(v):
    base = ((v & 8388607) + 8388608).astype(jnp.float32)
    negative = v >= 1073741824
    scale = jnp.exp2(((shr(v, 23) & 127) - 64).astype(jnp.float32))
    return base * jnp.where(negative, -scale, scale)


def int_of_word(x):
    size = jnp.abs(x)
    level = jnp.floor(jnp.log2(size) + 0.0009765625)
    value = size * jnp.exp2(23.0 - level)
    value = jnp.minimum(value, value + value - 8388608.0)
    offset = jnp.where(x < 0.0, jnp.int32((40 << 23) + (1 << 30)), jnp.int32(40 << 23))
    return value.astype(jnp.int32) + (level.astype(jnp.int32) << 23) + offset


def weighted_sum(limbs, weights):
    low = high = None
    for a, c in zip(limbs, weights):
        for n in range(3):
            low = a[n] * c[n] if low is None else low + a[n] * c[n]
            high = a[n] * c[3 + n] if high is None else high + a[n] * c[3 + n]
    return reduce_once(low + ((high & 32767) << 16) + shr(high, 15))


def degrees(a, b):
    return [
        a[0] * b[0],
        a[0] * b[1] + a[1] * b[0],
        a[0] * b[2] + a[1] * b[1] + a[2] * b[0],
        a[1] * b[2] + a[2] * b[1],
        a[2] * b[2],
    ]


def rotate(x, n):
    return ((x << n) & PRIME) + shr(x, 31 - n)


def element_of_degrees(d):
    total = add_mod(reduce_once(d[0]), rotate(d[1], 11))
    total = add_mod(total, rotate(d[2], 22))
    total = add_mod(total, rotate(d[3], 2))
    return add_mod(total, rotate(d[4], 13))


def mul_mod(a, b):
    return element_of_degrees(degrees(limbs_of(a), limbs_of(b)))


def add_limbs(a, b):
    return [x + y for x, y in zip(a, b)]


def nine_of(v):
    s02, s13 = add_limbs(v[0], v[2]), add_limbs(v[1], v[3])
    s01, s23 = add_limbs(v[0], v[1]), add_limbs(v[2], v[3])
    return [*v, s02, s13, s01, s23, add_limbs(s01, s23)]


MANY, ALL = range(8), range(9)


def clear(acc_ref, kinds):
    for kind in kinds:
        for n in range(5):
            acc_ref[5 * kind + n] = jnp.zeros((8, LANES), jnp.int32)


def two_rounds(acc_ref, weights_ref, phase, s, w):
    s, w = [[x if isinstance(x, tuple) else limbs_of(x) for x in v] for v in (s, w)]
    for kind, (a, b) in enumerate(zip(nine_of(s), nine_of(w))):
        for n, d in enumerate(degrees(a, b)):
            acc_ref[5 * kind + n] = acc_ref[5 * kind + n] + d
    weights = [[weights_ref[24 * phase + 6 * x + n] for n in range(6)] for x in range(4)]
    return weighted_sum(s, weights), weighted_sum(w, weights)


def flush(acc_ref, points_ref, first, kinds):
    for kind in kinds:
        here = element_of_degrees([acc_ref[5 * kind + n] for n in range(5)])
        points_ref[first + kind] = add_mod(points_ref[first + kind], here)


def over_pairs(count, tiles, accs, pair):
    assert tiles <= 16
    rare = [MANY if count * tiles <= 64 else () for _ in accs]

    def body(j, _):
        for (acc_ref, _, _), late in zip(accs, rare):
            clear(acc_ref, [k for k in ALL if k not in late])
        pair(j)
        for (acc_ref, points_ref, first), late in zip(accs, rare):
            flush(acc_ref, points_ref, first, [k for k in ALL if k not in late])

    for (acc_ref, _, _), late in zip(accs, rare):
        clear(acc_ref, late)
    lax.fori_loop(0, count, body, None)
    for (acc_ref, points_ref, first), late in zip(accs, rare):
        flush(acc_ref, points_ref, first, late)


def whole(scalar):
    return jnp.full((8, LANES), scalar, jnp.int32)


def sides(challenges_ref, place, phase):
    out = []
    for k in range(2):
        high = whole(challenges_ref[2 * phase + k])
        low = jnp.where(high == 0, 1, PRIME - high + 1)
        is_low = whole((place >> (1 - k)) & 1) == 0
        out.append((jnp.where(is_low, low, high), jnp.where(is_low, high, low)))
    return out


def constants_of(weight):
    parts = [weight, rotate(weight, 11), rotate(weight, 22)]
    return [x & 65535 for x in parts] + [shr(x, 16) for x in parts]


SQUARES, LOW_SIDE, WEIGHTS = 48, 84, 88


def place_of(axis):
    return lax.axis_index(axis) >> (lax.axis_size(axis).bit_length() - 3)


def weights_kernel(challenges_ref, weights_ref):
    for phase, axis in enumerate(("gx", "gy")):
        place = place_of(axis)
        first, second = sides(challenges_ref, place, phase)
        for x in range(4):
            for n, c in enumerate(constants_of(mul_mod(first[x >> 1], second[x & 1]))):
                weights_ref[24 * phase + 6 * x + n] = c
        own, other = first
        for x, pair in enumerate(((own, own), (own, other), (other, other))):
            for n, c in enumerate(constants_of(mul_mod(*pair))):
                weights_ref[SQUARES + 18 * phase + 6 * x + n] = c
        for k in range(2):
            weights_ref[LOW_SIDE + 2 * phase + k] = whole((place >> (1 - k)) & 1)


def tile(start, i):
    return pl.ds(pl.multiple_of(start + i * 8, 8), 8)


def over_tiles(rows, step):
    lax.fori_loop(0, rows // 8, step, None, unroll=min(UNROLL, rows // 8))


def item_of(table, item, quarter):
    parts = table.shape[4]
    return table.at[:, item // parts, quarter, :, item % parts]


def encode_kernel(raw, start, owns, s_hbm, w_hbm, *refs):
    tables = (s_hbm, w_hbm)
    gx, gy = place_of("gx"), place_of("gy")
    own_copies = []
    if len(owns):
        refs, own_sems = refs[:-1], refs[-1]
    buffer, sems = refs[-2:]
    refs = refs[:-2]
    if len(owns):
        refs, own_outs = refs[: -2 * len(owns)], refs[-2 * len(owns) :]
        own_copies = [
            pltpu.make_async_copy(item_of(tables[t], first + i, gx), own_outs[2 * n + t].at[:, i], own_sems.at[n, i, t])
            for n, (first, count) in enumerate(owns)
            for i in range(count)
            for t in range(2)
        ]
    token_ref = refs[-1]
    outs = refs[-5:-1] if raw else refs[-4:-1]
    count, rows = buffer.shape[0], buffer.shape[5]
    shifts = (1, 2, 3, 0) if raw else (1, 2, 3)
    order = [(i, d, t) for i in range(count) for d in shifts for t in range(2)]

    def copy(i, d, t):
        slot = d % len(shifts)
        return pltpu.make_async_copy(item_of(tables[t], start + i, gx ^ d), buffer.at[i, slot, t], sems.at[i, slot, t])

    for where in order:
        copy(*where).start()
    for copy_own in own_copies:
        copy_own.start()
    token_ref[...] = jnp.zeros_like(token_ref)
    for where in order:
        i, d, t = where
        copy(*where).wait()
        for e in range(4):
            src = gy ^ e if raw else e
            for k in range(rows // 8):
                at = pl.ds(8 * k, 8)
                word = word_of_limbs(*[buffer[i, d % len(shifts), t, n, src, at] for n in range(3)])
                if raw:
                    outs[e][t, i, d, at] = word
                else:
                    outs[d - 1][t, i, e, at] = word
    for copy_own in own_copies:
        copy_own.wait()


def gather_kernel(z0, z1, z2, z3, o1, o2, o3):
    for e, src in enumerate((z0, z1, z2, z3)):
        for d, out in enumerate((o1, o2, o3)):
            for t in range(2):
                for j in range(out.shape[1]):
                    out[t, j, e] = src[t, j, d + 1]


def first_kernel(fresh, weights_ref, s_ref, w_ref, g1, g2, g3, *refs):
    if not fresh:
        before_ref, *refs = refs
    points_ref, kept_ref, o1, o2, o3, acc_ref = refs
    count, rows = s_ref.shape[1], s_ref.shape[3]
    given, outs = (g1, g2, g3), (kept_ref, o1, o2, o3)
    gy = place_of("gy")
    points_ref[...] = jnp.zeros_like(points_ref) if fresh else before_ref[...]

    def pair(j):
        for e in range(4):
            src = gy ^ e

            def step(i, _):
                at = tile(0, i)
                values = []
                for t, own in enumerate((s_ref, w_ref)):
                    limbs = tuple(own[n, j, src, at].astype(jnp.int32) for n in range(3))
                    values.append([limbs] + [int_of_word(g[t, j, src, at]) for g in given])
                for t, folded in enumerate(two_rounds(acc_ref, weights_ref, 0, *values)):
                    outs[e][t, j, at] = word_of_int(folded) if e else folded

            over_tiles(rows, step)

    over_pairs(count, rows // 2, [(acc_ref, points_ref, 0)], pair)


def settle(lowest, middle, highest, passes=3):
    for _ in range(passes):
        carried = jnp.floor(lowest * (1.0 / 2048.0))
        lowest = lowest - carried * 2048.0
        middle = middle + carried
        carried = jnp.floor(middle * (1.0 / 2048.0))
        middle = middle - carried * 2048.0
        highest = highest + carried
        carried = jnp.floor(highest * (1.0 / 512.0))
        highest = highest - carried * 512.0
        lowest = lowest + carried
    if passes < 3:
        return lowest, middle, highest
    at_modulus = (lowest == 2047.0) & (middle == 2047.0) & (highest == 511.0)
    return [jnp.where(at_modulus, 0.0, limb) for limb in (lowest, middle, highest)]


def round_sums(weights_ref, phase, points):
    squares = [[weights_ref[SQUARES + 18 * phase + 6 * x + n] for n in range(6)] for x in range(3)]
    i0, i1, i2, i3, i02, i13, i01, i23, i0123 = points
    first = [add_mod(i0, i1), add_mod(i2, i3), add_mod(i02, i13)]
    second = []
    for own, other, both in ((i0, i2, i02), (i1, i3, i13), (i01, i23, i0123)):
        cross = sub_mod(both, add_mod(own, other))
        second.append(weighted_sum([limbs_of(x) for x in (own, cross, other)], squares))
    return [first, second]


def publish_row(weights_ref, points_ref, sums_ref):
    lane = lax.broadcasted_iota(jnp.int32, (1, LANES), 1)
    rows = [jnp.zeros((1, LANES), jnp.float32) for _ in range(3)]
    for phase in range(2):
        points = [points_ref[9 * phase + n] for n in range(9)]
        for k, (own, other, both) in enumerate(round_sums(weights_ref, phase, points)):
            is_low = weights_ref[LOW_SIDE + 2 * phase + k] == 0
            at_zero = jnp.where(is_low, own, other)
            at_one = jnp.where(is_low, other, own)
            once = add_mod(at_zero, add_mod(at_one, at_one))
            at_two = sub_mod(add_mod(once, add_mod(once, once)), add_mod(both, both))
            for t, value in enumerate((at_zero, at_one, at_two)):
                for n, limb in enumerate(limbs_of(value)):
                    total = jnp.sum(limb.astype(jnp.float32), axis=(0, 1), keepdims=True)
                    rows[n] = jnp.where(lane == 6 * phase + 3 * k + t, total, rows[n])
    low, mid, high = settle(*rows, passes=1)
    packed = low + pltpu.roll(mid, 16, 1) + pltpu.roll(high, 32, 1)
    sums_ref[...] = jnp.broadcast_to(packed, sums_ref.shape)


class Finish:
    def __init__(self, early, late, s_ref, w_ref, refs):
        self.sums_ref, s_hbm, w_hbm, sems = refs
        self.parts = [
            [
                pltpu.make_async_copy(src.at[:, part], dst.at[:, part], sems.at[which, t])
                for t, (src, dst) in enumerate(((s_ref, s_hbm), (w_ref, w_hbm)))
            ]
            for which, part in enumerate((pl.ds(*early), pl.ds(*late)))
        ]
        self.start(0)

    def start(self, which):
        for copy in self.parts[which]:
            copy.start()

    def end(self, weights_ref, points_ref):
        self.start(1)
        publish_row(weights_ref, points_ref, self.sums_ref)
        for copy in self.parts[0] + self.parts[1]:
            copy.wait()


def settle_kernel(sums_ref, out_ref):
    total = jnp.sum(sums_ref[...], axis=0)
    middle, highest = [pltpu.roll(total, LANES - n, 1) for n in (16, 32)]
    for n, limb in enumerate(settle(total, middle, highest)):
        for k in range(4):
            row = pltpu.roll(limb, LANES - 3 * k, 1) if k else limb
            out_ref[n, k : k + 1, :] = row[:, :3]


def put_folded(outs, j, at, folded):
    for out, value in zip(outs, folded):
        for n, limb in enumerate(limbs_of(jnp.where(value == PRIME, 0, value))):
            out[n, j, at] = limb.astype(jnp.float32)


def second_kernel(start, fresh, last, weights_ref, kept_ref, g1, g2, g3, before_ref, *refs):
    if not fresh:
        refs = refs[2:]
    points_ref, s_ref, w_ref, *refs = refs
    count, rows = kept_ref.shape[1], kept_ref.shape[2]
    if last:
        finish = Finish((0, start), (start, count), s_ref, w_ref, refs[:3] + refs[4:])
        refs = refs[3:4]
    (acc_ref,) = refs
    given = (g1, g2, g3)
    points_ref[...] = before_ref[...]

    def pair(j):
        def step(i, _):
            at = tile(0, i)
            s, w = [[kept_ref[t, j, at]] + [int_of_word(g[t, j, at]) for g in given] for t in range(2)]
            put_folded((s_ref, w_ref), start + j, at, two_rounds(acc_ref, weights_ref, 1, s, w))

        over_tiles(rows, step)

    over_pairs(count, rows // 8, [(acc_ref, points_ref, 9)], pair)
    if last:
        finish.end(weights_ref, points_ref)


def all_kernel(start, fresh, last, weights_ref, z0, z1, z2, z3, g1, g2, g3, before_ref, *refs):
    if not fresh:
        refs = refs[2:]
    points_ref, s_ref, w_ref, *refs = refs
    count, rows = z0.shape[1], z0.shape[3]
    if last:
        finish = Finish((0, start), (start, count), s_ref, w_ref, refs[:3] + refs[6:])
        refs = refs[3:6]
    acc_ref, acc2_ref, once = refs
    given = (g1, g2, g3)
    points_ref[...] = before_ref[...]

    def pair(j):
        for e, own in enumerate((z0, z1, z2, z3)):

            def step(i, _):
                at = tile(0, i)
                s, w = [[int_of_word(x) for x in [own[t, j, 0, at]] + [g[t, j, e, at] for g in given]] for t in range(2)]
                for t, folded in enumerate(two_rounds(acc_ref, weights_ref, 0, s, w)):
                    once[t, e, at] = folded

            over_tiles(rows, step)

        def step(i, _):
            at = tile(0, i)
            s, w = [[once[t, e, at] for e in range(4)] for t in range(2)]
            put_folded((s_ref, w_ref), start + j, at, two_rounds(acc2_ref, weights_ref, 1, s, w))

        over_tiles(rows, step)

    over_pairs(count, rows // 2, [(acc_ref, points_ref, 0), (acc2_ref, points_ref, 9)], pair)
    if last:
        finish.end(weights_ref, points_ref)


def swap_with(x, axis, mask):
    return lax.ppermute(x, axis, [(i, i ^ mask) for i in range(lax.axis_size(axis))])


SPLIT = 1
CHUNKS, RAW = (4, 2), 2
SENDS = "0R1"
STEPS = ("A0", "G", "A1", "B0", "K", "B1")
POINTS = pltpu.VMEM((18, 8, LANES), jnp.int32)


def plan(items):
    if sum(CHUNKS) + RAW == items:
        return CHUNKS, RAW, SENDS, STEPS
    steps = ["A0"] + [x for c in range(1, items) for x in (f"A{c}", f"B{c - 1}")] + [f"B{items - 1}"]
    return (1,) * items, 0, range(items), steps


def shards(devices, selectors, proofs, challenges):
    polynomials, row_count = selectors.shape[1], selectors.shape[-1]
    lane_rows = row_count // LANES
    parts = SPLIT if lane_rows % (128 * SPLIT) == 0 else 1
    items, final = polynomials * parts, lane_rows // 16 // parts
    shape = (3, polynomials, 4, 4, parts, final, LANES)
    tables = [pltpu.with_memory_space_constraint(x.reshape(shape), pltpu.HBM) for x in (selectors, proofs)]
    gx_shift = lax.axis_size("gx").bit_length() - 3
    gy_shift = lax.axis_size("gy").bit_length() - 3

    sizes, raw, sends, steps = plan(items)
    raw_last = steps[-1] == "K"
    raw_start = items - raw if raw_last else 0
    starts = [sum(sizes[:c]) + (0 if raw_last else raw) for c in range(len(sizes))]
    smem, vmem, hbm, anywhere = [pl.BlockSpec(memory_space=m) for m in (pltpu.SMEM, pltpu.VMEM, pltpu.HBM, pl.ANY)]

    def words(count, rows, dtype=jnp.float32):
        return pltpu.VMEM((2, count, *rows, LANES), dtype)

    def near(arrays):
        return [pltpu.with_memory_space_constraint(x, pltpu.VMEM) for x in arrays]

    work = [pltpu.VMEM((45, 8, LANES), jnp.int32)]
    small = pltpu.CompilerParams(vmem_limit_bytes=VMEM_KERNEL)

    def encode(raw_chunk, start, count, outs, owns, token):
        out_shape = outs + [pltpu.VMEM((8, LANES), jnp.float32)]
        out_shape += [pltpu.VMEM((3, n, 4, final, LANES), jnp.float32) for _, n in owns for _ in range(2)]
        shifts = 4 if raw_chunk else 3
        scratch = [
            pltpu.VMEM((count, shifts, 2, 3, 4, final, LANES), jnp.float32),
            pltpu.SemaphoreType.DMA((count, shifts, 2)),
        ]
        if owns:
            scratch.append(pltpu.SemaphoreType.DMA((len(owns), max(n for _, n in owns), 2)))
        return pl.pallas_call(
            functools.partial(encode_kernel, raw_chunk, start, owns),
            in_specs=[hbm, hbm] + [anywhere] * len(token),
            out_specs=[vmem] * len(out_shape),
            out_shape=out_shape,
            scratch_shapes=scratch,
            compiler_params=pltpu.CompilerParams(vmem_limit_bytes=VMEM_ENCODE),
            name="encode",
        )(*tables, *token)

    def first(c, own, given, before):
        count = sizes[c]
        fresh = before is None
        return pl.pallas_call(
            functools.partial(first_kernel, fresh),
            in_specs=[vmem] * (6 if fresh else 7),
            out_specs=[vmem] * 5,
            out_shape=[POINTS, words(count, [final], jnp.int32)] + [words(count, [final])] * 3,
            scratch_shapes=work,
            input_output_aliases={} if fresh else {6: 0},
            compiler_params=small,
            name="first_rounds",
        )(weights, *own, *near(given), *(() if fresh else (before,)))

    def fold_last(kernel, start, arrays, before, folded, last, scratch):
        fresh = folded is None
        shape = (3, items, final, LANES)
        out_shape, out_specs = [POINTS] + [pltpu.VMEM(shape, jnp.float32)] * 2, [vmem] * 3
        if last:
            out_shape += [jax.ShapeDtypeStruct((devices, 1, LANES), jnp.float32)] + [jax.ShapeDtypeStruct(shape, jnp.float32)] * 2
            out_specs += [vmem, hbm, hbm]
            scratch = scratch + [pltpu.SemaphoreType.DMA((2, 2))]
        at = 1 + len(arrays)
        return pl.pallas_call(
            functools.partial(kernel, start, fresh, last),
            in_specs=[vmem] * (len(arrays) + (2 if fresh else 4)),
            out_specs=out_specs,
            out_shape=out_shape,
            scratch_shapes=scratch,
            input_output_aliases={at: 0} if fresh else {at: 0, at + 1: 1, at + 2: 2},
            compiler_params=small,
        )(weights, *near(arrays), before, *(() if fresh else folded))

    def swap(arrays, axis, shift):
        return [swap_with(x, axis, (d + 1) << shift) for d, x in enumerate(arrays)]

    owns, sent, token = {}, {}, []
    reader = list(sends)[min(1, len(sends) - 1)]
    ranges = list(zip(starts, sizes))
    for c in sends:
        raw_chunk = c == "R"
        if raw_chunk:
            start, count, outs = raw_start, raw, [words(raw, [4, final])] * 4
        else:
            start, count = ranges[int(c)]
            outs = [words(count, [4, final])] * 3
        out = encode(raw_chunk, start, count, outs, ranges if c == reader else [], token)
        given, token = out[: len(outs)], [out[len(outs)]]
        if raw_chunk:
            raw_own, *given = given
        if c == reader:
            rest = out[len(outs) + 1 :]
            owns = {n: rest[2 * n : 2 * n + 2] for n in range(len(ranges))}
        sent[c if raw_chunk else int(c)] = swap(given, *(("gy", gy_shift) if raw_chunk else ("gx", gx_shift)))
    weights = pl.pallas_call(
        weights_kernel,
        in_specs=[smem],
        out_specs=vmem,
        out_shape=pltpu.VMEM((WEIGHTS, 8, LANES), jnp.int32),
        compiler_params=small,
        name="weights",
    )(challenges)
    points, folded, waiting = None, None, {}
    for step in steps:
        last = step == steps[-1]
        c = int(step[1:] or 0)
        if step[0] == "A":
            points, kept, *given = first(c, owns[c], sent[c], points)
        elif step[0] == "G":
            around = [raw_own, *sent["R"]]
            given = pl.pallas_call(
                gather_kernel,
                in_specs=[vmem] * 4,
                out_specs=[vmem] * 3,
                out_shape=[words(raw, [4, final])] * 3,
                compiler_params=small,
                name="gather",
            )(*near(around))
        elif step[0] == "K":
            scratch = work + work + [pltpu.VMEM((2, 4, final, LANES), jnp.int32)]
            points, *folded = fold_last(all_kernel, raw_start, around + given_raw, points, folded, last, scratch)
        else:
            points, *folded = fold_last(second_kernel, starts[c], waiting[c], points, folded, last, work)
        if step[0] == "A":
            waiting[c] = [kept, *swap(given, "gy", gy_shift)]
        elif step[0] == "G":
            given_raw = swap(given, "gx", gx_shift)
    sums, *folded = folded[2:]
    gathered = lax.all_to_all(sums, ("gx", "gy"), 0, 0)
    points = pl.pallas_call(
        settle_kernel,
        in_specs=[vmem],
        out_specs=vmem,
        out_shape=jax.ShapeDtypeStruct((3, 4, 3), jnp.float32),
        compiler_params=small,
        name="settle",
    )(gathered)
    shape = (3, polynomials, 1, 1, row_count // 16)
    return points, folded[0].reshape(shape), folded[1].reshape(shape)


def solution(mesh):
    tables = P(None, None, "gx", "gy", None)
    devices = mesh.shape["gx"] * mesh.shape["gy"]

    def body(*arrays):
        return shards(devices, *arrays)

    return jax.shard_map(
        body,
        mesh=mesh,
        in_specs=(tables, tables, P()),
        out_specs=(P(), tables, tables),
        check_vma=False,
    )
```
